1024 devices in a mesh: member: 32 (over y_lo, z), patch: 32 (over x, y_hi, core).
Axes of the slice: x: 8, y: 8 (y_hi: 2, y_lo: 4; y = y_hi * 4 + y_lo), z: 8, core: 2. Of those that a mesh axis runs over, the one named last changes fastest.
Arguments:
- control: float32 [96, 8, 65536], P('member', None, 'patch'), may hold values from -6 to 6
- members: bfloat16 [96, 8, 262144], P('member', None, 'patch'), may hold values from -6 to 6
- conv_blocks: bfloat16 [3, 512, 128, 128], P(None, 'patch'), may hold values from -0.3125 to 0.3125
- interp_weights: bfloat16 [2048, 128, 128], P('patch'), may hold values from -0.5 to 0.5
- interp_source: int32 [2048], P('patch'), may hold values from 0 to 15
- right_rows: int32 [32, 128], P('patch'), may hold values from 1792 to 2047
- left_rows: int32 [32, 128], P('patch'), may hold values from 0 to 255
- obs_cells: int32 [32, 32768], P('patch', 'member'), may hold values from 0 to 255
- obs_weights: float32 [32, 8, 32768], P('patch', None, 'member'), may hold values from -2 to 2
- obs_precision: float32 [32, 32768], P('patch', 'member'), may hold values from 1 to 16
- obs_count: int32 [32, 32], P('patch', 'member'), may hold values from 128 to 1024
Outputs:
- hessian_product: float32 [96, 8, 65536], P('member', None, 'patch')
- increment: float32 [8, 262144], P(None, ('patch', 'member'))
The draws below stay inside these ranges and needn't reach their ends.
Inputs may be any that keep to these rules, and one draw needn't show every extreme that they name: `right_rows`: indices into the nodes of the same patch, among its last 256. `left_rows`: indices into the nodes of the same patch, among its first 256.
All inputs are finite; a program needn't handle non-finite values.
Results may differ from the reference program's by a relative error of at most 0.0055.
Values may be sent and summed in bfloat16 or wider, within the bound.
A program may use at most 64 MiB of HBM per device.

```python
import math
import jax
import jax.numpy as jnp
from jax import lax

LEV = 8
BLOCK = 128
NBLK_DEV = 16
CBLK_DEV = 64
OBS_DEV = 1024
MEMBERS = 96
NODES_DEV = 2048
CELLS_DEV = 8192
NODES = 65536
CELLS = 262144
NBLOCKS = 512
CBLOCKS = 2048
OBS_PATCH = 32768
N_MEMBER = 32
N_PATCH = 32


def place_ends(values, key, smallest, largest):
    place = [jax.random.randint(jax.random.fold_in(key, axis), (), 0, length) for axis, length in enumerate(values.shape)]
    longest = values.shape.index(max(values.shape))
    beside = place[:longest] + [(place[longest] + 1) % values.shape[longest]] + place[longest + 1:]
    return values.at[tuple(place)].set(smallest).at[tuple(beside)].set(largest)


def block_scale(own_key, extent, cuts, least, high):
    factor_of = 1.0
    for axis_at, parts in cuts:
        steps = jax.random.uniform(jax.random.fold_in(jax.random.fold_in(own_key, 6), axis_at), (parts,), jnp.float32, least / len(cuts), high / len(cuts))
        factor_of = factor_of * jnp.repeat(jnp.exp(steps), extent[axis_at] // parts).reshape((-1,) + (1,) * (len(extent) - 1 - axis_at))
    return factor_of


def normal_values(stream_key, shape, scale, bound, shards=(), held_as=jnp.bfloat16):
    values = scale * jax.random.normal(stream_key, shape, jnp.float32)
    if shards:
        values = values * block_scale(stream_key, shape, shards, -0.22, 0.18)
    return jnp.clip(values, -bound, bound).astype(held_as)


def setup_inputs(seed: int = 0) -> dict:
    splits = jax.random.split(jax.random.key(seed), 12)
    return {
        "control": normal_values(splits[0], (MEMBERS, LEV, NODES), 1.0, 6.0, ((0, 32), (2, 32)), jnp.float32),
        "members": normal_values(splits[1], (MEMBERS, LEV, CELLS), 1.0, 6.0, ((0, 32), (2, 32))),
        "conv_blocks": normal_values(splits[2], (3, NBLOCKS, BLOCK, BLOCK), (3 * BLOCK) ** -0.5, 0.3125, ((1, 32),)),
        "interp_weights": normal_values(splits[3], (CBLOCKS, BLOCK, BLOCK), BLOCK ** -0.5, 0.5, ((0, 32),)),
        "interp_source": place_ends(jax.random.randint(splits[4], (CBLOCKS,), 0, NBLK_DEV), jax.random.fold_in(splits[4], 1), 0, NBLK_DEV - 1).astype(jnp.int32),
        "right_rows": place_ends(jax.random.randint(splits[5], (N_PATCH, BLOCK), NODES_DEV - 2 * BLOCK, NODES_DEV), jax.random.fold_in(splits[5], 1), NODES_DEV - 2 * BLOCK, NODES_DEV - 1).astype(jnp.int32),
        "left_rows": place_ends(jax.random.randint(splits[6], (N_PATCH, BLOCK), 0, 2 * BLOCK), jax.random.fold_in(splits[6], 1), 0, (2 * BLOCK) - 1).astype(jnp.int32),
        "obs_cells": place_ends(jax.random.randint(splits[7], (N_PATCH, OBS_PATCH), 0, CELLS_DEV // N_MEMBER), jax.random.fold_in(splits[7], 1), 0, (CELLS_DEV // N_MEMBER) - 1).astype(jnp.int32),
        "obs_weights": normal_values(splits[8], (N_PATCH, LEV, OBS_PATCH), LEV ** -0.5, 2.0, ((0, 32), (2, 32)), jnp.float32),
        "obs_precision": jnp.clip(jnp.exp(math.log(16.0) - 2.7725887 * jax.random.uniform(splits[9], (N_PATCH, OBS_PATCH), jnp.float32) ** block_scale(splits[9], (N_PATCH, OBS_PATCH), ((0, 32), (1, 32)), -0.2, 0.2)), 1.0, 16.0),
        "obs_count": place_ends(jax.random.randint(splits[10], (N_PATCH, N_MEMBER), OBS_DEV // 8, OBS_DEV + 1), jax.random.fold_in(splits[10], 1), OBS_DEV // 8, OBS_DEV).astype(jnp.int32),
    }


def widen(array):
    return array.astype(jnp.float32)

def conv_patch(node_blocks, earlier, later, kernels):
    result = jnp.einsum('rbn,bmn->rbm', widen(node_blocks), widen(kernels[0]))
    result = result + jnp.einsum('rbn,bmn->rbm', widen(earlier), widen(kernels[1]))
    return result + jnp.einsum('rbn,bmn->rbm', widen(later), widen(kernels[2]))

def reference(control, members, conv_blocks, interp_weights, interp_source, right_rows, left_rows, obs_cells, obs_weights, obs_precision, obs_count):
    total_rows = MEMBERS * LEV
    factor = 1.0 / math.sqrt(MEMBERS - 1)
    rounded = control.astype(jnp.bfloat16).reshape(total_rows, N_PATCH, NODES_DEV)
    sent_right = jnp.take_along_axis(rounded, right_rows[None], axis=2)
    sent_left = jnp.take_along_axis(rounded, left_rows[None], axis=2)
    lower_halo = jnp.roll(sent_right, 1, axis=1)
    upper_halo = jnp.roll(sent_left, -1, axis=1)
    node_blocks = rounded.reshape(total_rows, N_PATCH, NBLK_DEV, BLOCK)
    earlier = jnp.concatenate([lower_halo[:, :, None], node_blocks[:, :, :-1]], axis=2)
    later = jnp.concatenate([node_blocks[:, :, 1:], upper_halo[:, :, None]], axis=2)
    kernels = jnp.moveaxis(conv_blocks.reshape(3, N_PATCH, NBLK_DEV, BLOCK, BLOCK), 1, 0)
    weights = interp_weights.reshape(N_PATCH, CBLK_DEV, BLOCK, BLOCK)
    sources = interp_source.reshape(N_PATCH, CBLK_DEV)
    perturb = jnp.moveaxis(members.reshape(MEMBERS, LEV, N_PATCH, CELLS_DEV), 2, 0)

    def forward(packed):
        blocks_p, earlier_p, later_p, kernels_p, weights_p, sources_p, perturb_p = packed
        conv = conv_patch(blocks_p, earlier_p, later_p, kernels_p).astype(jnp.bfloat16)
        picked = jnp.take(conv, sources_p, axis=1)
        field = jnp.einsum('rcn,cmn->rcm', widen(picked), widen(weights_p)).reshape(MEMBERS, LEV, CELLS_DEV)
        return lax.optimization_barrier(jnp.sum(field * widen(perturb_p), axis=0)) * factor
    patch_incs = lax.map(forward, (jnp.moveaxis(node_blocks, 1, 0), jnp.moveaxis(earlier, 1, 0), jnp.moveaxis(later, 1, 0), kernels, weights, sources, perturb))
    increment = jnp.moveaxis(patch_incs, 0, 1).reshape(LEV, N_PATCH * CELLS_DEV)
    cells_own = CELLS_DEV // N_MEMBER
    slots = jnp.arange(N_MEMBER * OBS_DEV, dtype=jnp.int32)
    owner = slots // OBS_DEV
    live = ((slots % OBS_DEV)[None, :] < obs_count[:, owner]).astype(jnp.float32)
    places = jnp.arange(N_PATCH, dtype=jnp.int32)[:, None] * CELLS_DEV + owner[None, :] * cells_own + obs_cells
    flat_places = places.reshape(-1)
    level_weights = jnp.moveaxis(obs_weights, 1, 0).reshape(LEV, -1)
    evolved = lax.optimization_barrier(jnp.sum(level_weights * increment[:, flat_places], axis=0))
    departure = obs_precision.reshape(-1) * evolved * live.reshape(-1)
    sensitivity = jnp.zeros((LEV, N_PATCH * CELLS_DEV), jnp.float32).at[:, flat_places].add(level_weights * departure[None, :])
    sens_patch = jnp.moveaxis(sensitivity.astype(jnp.bfloat16).reshape(LEV, N_PATCH, CELLS_DEV), 1, 0)

    def backward(packed):
        sens_p, kernels_p, weights_p, sources_p, perturb_p = packed
        adjoint = (widen(perturb_p) * widen(sens_p)[None] * factor).astype(jnp.bfloat16).reshape(total_rows, CBLK_DEV, BLOCK)
        spread = jnp.einsum('rcm,cmn->rcn', widen(adjoint), widen(weights_p))
        chooser = (sources_p[:, None] == jnp.arange(NBLK_DEV, dtype=jnp.int32)[None, :]).astype(jnp.float32)
        nodal = jnp.einsum('rcn,cb->rbn', spread, chooser, precision=lax.Precision.HIGHEST).astype(jnp.bfloat16)
        own_part = jnp.einsum('rbm,bmn->rbn', widen(nodal), widen(kernels_p[0]))
        back_part = jnp.einsum('rbm,bmn->rbn', widen(nodal), widen(kernels_p[1]))
        ahead_part = jnp.einsum('rbm,bmn->rbn', widen(nodal), widen(kernels_p[2]))
        zeros_blk = jnp.zeros_like(own_part[:, :1])
        summed = own_part + jnp.concatenate([back_part[:, 1:], zeros_blk], axis=1) + jnp.concatenate([zeros_blk, ahead_part[:, :-1]], axis=1)
        return (summed.reshape(total_rows, NODES_DEV), back_part[:, 0], ahead_part[:, -1])
    summed, to_lower, to_upper = lax.map(backward, (sens_patch, kernels, weights, sources, perturb))
    from_upper = jnp.roll(to_lower, -1, axis=0)
    from_lower = jnp.roll(to_upper, 1, axis=0)

    def settle(total_p, rows_r, rows_l, add_r, add_l):
        return total_p.at[:, rows_r].add(add_r).at[:, rows_l].add(add_l)
    summed = jax.vmap(settle)(summed, right_rows, left_rows, from_upper, from_lower)
    back = jnp.transpose(summed.reshape(N_PATCH, MEMBERS, LEV, NODES_DEV), (1, 2, 0, 3)).reshape(MEMBERS, LEV, N_PATCH * NODES_DEV)
    return (control + back, increment)
```

```python
import functools
import math

import jax
import jax.numpy as jnp
from jax import lax
from jax.experimental import pallas as pl
from jax.experimental.pallas import tpu as pltpu
from jax.sharding import PartitionSpec as P

F32 = jnp.float32
BF16 = jnp.bfloat16
LANES = 128
MESH = pl.DeviceIdType.MESH


def dot_nt(x, w):
    return lax.dot_general(x, w, (((1,), (1,)), ((), ())), preferred_element_type=F32)


def dot_nn(x, w):
    return lax.dot_general(x, w, (((1,), (0,)), ((), ())), preferred_element_type=F32)


def table(rows, base, count):
    node = lax.broadcasted_iota(jnp.int32, (count, rows.shape[1]), 0) + base
    return jnp.where(node == rows, 1.0, 0.0).astype(BF16)


def split_bf16(x):
    high = x.astype(BF16)
    return high, (x - high.astype(F32)).astype(BF16)


def kernel(
    groups,
    depth,
    patches,
    control_h,
    members_h,
    conv_h,
    interp_h,
    source_h,
    right_h,
    left_h,
    cells_h,
    weights_h,
    precision_h,
    count_h,
    product_h,
    inc_h,
    control_v,
    members_v,
    conv_v,
    interp_v,
    source_s,
    right_v,
    left_v,
    cells_v,
    weights_v,
    precision_v,
    count_s,
    load_sem,
    right_table,
    left_table,
    halo_send,
    halo_recv,
    halo_send_sem,
    halo_recv_sem,
    edge_acc,
    conv_f,
    obs_a,
    part,
    arrived,
    part_send_sem,
    part_recv_sem,
    inc_v,
    sens,
    sens_send_sem,
    sens_recv_sem,
    nodal,
    give,
    got,
    give_send_sem,
    give_recv_sem,
    product_v,
    out_sem,
):
    me = lax.axis_index("member")
    patch = lax.axis_index("patch")
    width = groups // depth
    my_row, my_col = me // depth, lax.rem(me, depth)
    upper, lower = lax.rem(patch + 1, patches), lax.rem(patch + patches - 1, patches)
    mem_here, levels, node_count = control_v.shape
    rows = mem_here * levels
    blocks = node_count // LANES
    edge = 2 * LANES
    factor = 1.0 / math.sqrt(mem_here * groups - 1)
    near = sorted(range(depth), key=lambda d: (min(d, depth - d), d))
    far = near[::-1]

    def peer(turn, step):
        return lax.rem(my_row + turn, width) * depth + lax.rem(my_col + step, depth)

    def each_turn(body):
        lax.fori_loop(0, width, lambda t, carry: (body(t), carry)[1], 0)

    def unless_me(turn, step, act):
        if step == 0:
            pl.when(turn > 0)(act)
        else:
            act()

    barrier = pltpu.get_barrier_semaphore()

    def greet(turn):
        for step in far:
            unless_me(
                turn,
                step,
                lambda: pl.semaphore_signal(
                    barrier, inc=1, device_id=(peer(turn, step), patch), device_id_type=MESH
                ),
            )

    for other in (upper, lower):
        pl.semaphore_signal(barrier, inc=1, device_id=(me, other), device_id_type=MESH)
    each_turn(greet)

    sources = (control_h, right_h, left_h, source_h, conv_h, weights_h, precision_h, cells_h, count_h, interp_h, members_h)
    targets = (control_v, right_v, left_v, source_s, conv_v, weights_v, precision_v, cells_v, count_s, interp_v, members_v)
    loads = [
        pltpu.make_async_copy(a, b, load_sem.at[i]) for i, (a, b) in enumerate(zip(sources, targets))
    ]
    for load in loads:
        load.start()

    def node_block(b):
        return control_v[:, :, b * LANES : (b + 1) * LANES].reshape(rows, LANES).astype(BF16)

    for load in loads[:3]:
        load.wait()
    right_table[...] = table(right_v[...], node_count - edge, edge)
    left_table[...] = table(left_v[...], 0, edge)
    last = jnp.concatenate([node_block(blocks - 2), node_block(blocks - 1)], axis=1)
    first = jnp.concatenate([node_block(0), node_block(1)], axis=1)
    halo_send[0] = dot_nn(last, right_table[...]).astype(BF16)
    halo_send[1] = dot_nn(first, left_table[...]).astype(BF16)

    pl.semaphore_wait(barrier, groups + 1)

    def halo_copy(i, other):
        return pltpu.make_async_remote_copy(
            src_ref=halo_send.at[i],
            dst_ref=halo_recv.at[i],
            send_sem=halo_send_sem.at[i],
            recv_sem=halo_recv_sem.at[i],
            device_id=(me, other),
            device_id_type=MESH,
        )

    halos = [halo_copy(0, upper), halo_copy(1, lower)]
    for copy in halos:
        copy.start()

    for load in loads[3:5]:
        load.wait()
    for b in range(blocks):
        acc = dot_nt(node_block(b), conv_v[0, b])
        if b > 0:
            acc = acc + dot_nt(node_block(b - 1), conv_v[1, b])
        if b < blocks - 1:
            acc = acc + dot_nt(node_block(b + 1), conv_v[2, b])
        if b == 0:
            edge_acc[0] = acc
        elif b == blocks - 1:
            edge_acc[1] = acc
        else:
            conv_f[b] = acc.astype(BF16).astype(F32)

    for load in loads[5:9]:
        load.wait()
    slots = cells_v.shape[1]
    own = 2 * LANES
    live = lax.broadcasted_iota(jnp.int32, (1, slots), 1) < count_s[0, 0]
    scaled = jnp.where(live, precision_v[...], 0.0)
    level_w = weights_v[0]
    outer = jnp.concatenate(
        [level_w * (level_w[l : l + 1] * scaled) for l in range(levels)], axis=0
    )
    place = table(cells_v[...], 0, own)
    high, low = split_bf16(outer)
    obs_a[...] = dot_nt(high, place) + dot_nt(low, place)

    for load in loads[9:]:
        load.wait()
    for copy in halos:
        copy.wait_recv()
    conv_f[0] = (edge_acc[0] + dot_nt(halo_recv[0], conv_v[1, 0])).astype(BF16).astype(F32)
    conv_f[blocks - 1] = (
        (edge_acc[1] + dot_nt(halo_recv[1], conv_v[2, blocks - 1])).astype(BF16).astype(F32)
    )

    def members_at(c):
        here = members_v[:, :, pl.ds(pl.multiple_of(c * LANES, LANES), LANES)]
        return here.astype(F32)

    def part_copy(m, landing):
        return pltpu.make_async_remote_copy(
            src_ref=part.at[m],
            dst_ref=arrived.at[landing],
            send_sem=part_send_sem.at[m],
            recv_sem=part_recv_sem.at[landing],
            device_id=(m, patch),
            device_id_type=MESH,
        )

    def forward(t):
        turn = width - 1 - t
        for step in far:
            m = peer(turn, step)
            halves = []
            for h in range(2):
                c = m * 2 + h
                picked = conv_f[source_s[c]].astype(BF16)
                field = dot_nt(picked, interp_v[c]).reshape(mem_here, levels, LANES)
                halves.append(jnp.sum(field * members_at(c), axis=0))
            part[m] = jnp.concatenate(halves, axis=0).astype(BF16)
        for step in far:
            unless_me(turn, step, lambda: part_copy(peer(turn, step), me).start())

    each_turn(forward)

    arrived[me] = part[me]

    def take_in(t, total):
        for step in near:
            m = peer(t, step)
            unless_me(t, step, lambda: part_copy(m, m).wait_recv())
            total = total + arrived[m].astype(F32)
        return total

    total = lax.fori_loop(0, width, take_in, jnp.zeros((2 * levels, LANES), F32))
    inc = total * factor

    pieces = []
    for h in range(2):
        half = inc[h * levels : (h + 1) * levels]
        inc_v[:, h * LANES : (h + 1) * LANES] = half
        acc = None
        for l in range(levels):
            term = (
                obs_a[l * levels : (l + 1) * levels, h * LANES : (h + 1) * LANES]
                * half[l : l + 1]
            )
            acc = term if acc is None else acc + term
        pieces.append(acc)
    sens[me] = jnp.concatenate(pieces, axis=0).astype(BF16)

    def sens_copy(m, landing):
        return pltpu.make_async_remote_copy(
            src_ref=sens.at[landing],
            dst_ref=sens.at[landing],
            send_sem=sens_send_sem.at[m],
            recv_sem=sens_recv_sem.at[landing],
            device_id=(m, patch),
            device_id_type=MESH,
        )

    def share(t):
        turn = width - 1 - t
        for step in far:
            unless_me(turn, step, lambda: sens_copy(peer(turn, step), me).start())

    each_turn(share)
    inc_out = pltpu.make_async_copy(inc_v, inc_h, out_sem.at[0])
    inc_out.start()
    nodal[...] = jnp.zeros_like(nodal)

    def backward(turn):
        for pair in range(0, depth, 2):
            spread = []
            for step in near[pair : pair + 2]:
                m = peer(turn, step)
                unless_me(turn, step, lambda: sens_copy(m, m).wait_recv())
                there = sens[m].astype(F32) * factor
                for h in range(2):
                    c = m * 2 + h
                    adjoint = members_at(c) * there[h * levels : (h + 1) * levels][None]
                    adjoint = adjoint.reshape(rows, LANES).astype(BF16)
                    at = jnp.full((rows, LANES), source_s[c], jnp.int32)
                    spread.append((at, dot_nn(adjoint, interp_v[c])))
            for b in range(blocks):
                acc = nodal[b]
                for at, value in spread:
                    acc = acc + jnp.where(at == b, value, 0.0)
                nodal[b] = acc

    each_turn(backward)

    def give_copy(i, other):
        return pltpu.make_async_remote_copy(
            src_ref=give.at[i],
            dst_ref=got.at[i],
            send_sem=give_send_sem.at[i],
            recv_sem=give_recv_sem.at[i],
            device_id=(me, other),
            device_id_type=MESH,
        )

    def node_adjoint(b):
        return nodal[b].astype(BF16)

    give[0] = dot_nn(node_adjoint(0), conv_v[1, 0]).astype(BF16)
    give[1] = dot_nn(node_adjoint(blocks - 1), conv_v[2, blocks - 1]).astype(BF16)
    gifts = [give_copy(0, lower), give_copy(1, upper)]
    for copy in gifts:
        copy.start()

    for b in range(blocks):
        acc = dot_nn(node_adjoint(b), conv_v[0, b])
        if b < blocks - 1:
            acc = acc + dot_nn(node_adjoint(b + 1), conv_v[1, b + 1])
        if b > 0:
            acc = acc + dot_nn(node_adjoint(b - 1), conv_v[2, b - 1])
        span = slice(b * LANES, (b + 1) * LANES)
        product_v[:, :, span] = control_v[:, :, span] + acc.reshape(mem_here, levels, LANES)

    inner = pl.ds(edge, node_count - 2 * edge)
    inner_out = pltpu.make_async_copy(
        product_v.at[:, :, inner], product_h.at[:, :, inner], out_sem.at[1]
    )
    inner_out.start()

    outs = [inc_out, inner_out]
    for i, (tab, start) in enumerate(((right_table, node_count - edge), (left_table, 0))):
        gifts[i].wait_recv()
        added = dot_nt(got[i], tab[...]).reshape(mem_here, levels, edge)
        span = slice(start, start + edge)
        product_v[:, :, span] = product_v[:, :, span] + added
        out = pltpu.make_async_copy(
            product_v.at[:, :, pl.ds(start, edge)],
            product_h.at[:, :, pl.ds(start, edge)],
            out_sem.at[2 + i],
        )
        out.start()
        outs.append(out)

    for copy in halos + gifts:
        copy.wait_send()

    def drain(turn):
        for step in near:
            m = peer(turn, step)

            def sent():
                part_copy(m, me).wait_send()
                sens_copy(m, me).wait_send()

            unless_me(turn, step, sent)

    each_turn(drain)
    for out in outs:
        out.wait()


def per_device(*args):
    control, members, conv_blocks, interp = args[:4]
    groups, patches = lax.axis_size("member"), lax.axis_size("patch")
    depth = 8 if groups % 8 == 0 else 2
    mem_here, levels, node_count = control.shape
    rows = mem_here * levels
    blocks = node_count // LANES
    slots = args[7].shape[1]
    own = 2 * LANES
    smem = (4, 10)
    loaded = [
        (pltpu.SMEM if i in smem else pltpu.VMEM)(a.shape, a.dtype) for i, a in enumerate(args)
    ]
    dma = pltpu.SemaphoreType.DMA
    piece = (groups, 2 * levels, LANES)
    out_shape = (
        jax.ShapeDtypeStruct(control.shape, F32),
        jax.ShapeDtypeStruct((levels, own), F32),
    )
    return pl.pallas_call(
        functools.partial(kernel, groups, depth, patches),
        out_shape=out_shape,
        in_specs=[pl.BlockSpec(memory_space=pltpu.HBM)] * len(args),
        out_specs=[pl.BlockSpec(memory_space=pltpu.HBM)] * 2,
        scratch_shapes=loaded
        + [
            dma((len(args),)),
            pltpu.VMEM((own, LANES), BF16),
            pltpu.VMEM((own, LANES), BF16),
            pltpu.VMEM((2, rows, LANES), BF16),
            pltpu.VMEM((2, rows, LANES), BF16),
            dma((2,)),
            dma((2,)),
            pltpu.VMEM((2, rows, LANES), F32),
            pltpu.VMEM((blocks, rows, LANES), F32),
            pltpu.VMEM((levels * levels, own), F32),
            pltpu.VMEM(piece, BF16),
            pltpu.VMEM(piece, BF16),
            dma((groups,)),
            dma((groups,)),
            pltpu.VMEM((levels, own), F32),
            pltpu.VMEM(piece, BF16),
            dma((groups,)),
            dma((groups,)),
            pltpu.VMEM((blocks, rows, LANES), F32),
            pltpu.VMEM((2, rows, LANES), BF16),
            pltpu.VMEM((2, rows, LANES), BF16),
            dma((2,)),
            dma((2,)),
            pltpu.VMEM(control.shape, F32),
            dma((4,)),
        ],
        compiler_params=pltpu.CompilerParams(collective_id=0, has_side_effects=True),
        name="hessian_step",
    )(*args)


def solution(mesh):
    placed = (
        P("member", None, "patch"),
        P("member", None, "patch"),
        P(None, "patch", None, None),
        P("patch", None, None),
        P("patch"),
        P("patch", None),
        P("patch", None),
        P("patch", "member"),
        P("patch", None, "member"),
        P("patch", "member"),
        P("patch", "member"),
    )
    return jax.shard_map(
        per_device,
        mesh=mesh,
        in_specs=placed,
        out_specs=(P("member", None, "patch"), P(None, ("patch", "member"))),
        check_vma=False,
    )
```

```python
import functools
import math

import jax
import jax.numpy as jnp
from jax import lax
from jax.experimental import pallas as pl
from jax.experimental.pallas import tpu as pltpu
from jax.sharding import PartitionSpec as P

F32 = jnp.float32
BF16 = jnp.bfloat16
LANES = 128
VMEM_GRANT = 48 << 20
MESH = pl.DeviceIdType.MESH


def dot_nt(x, w):
    return lax.dot_general(x, w, (((1,), (1,)), ((), ())), preferred_element_type=F32)


def dot_nn(x, w):
    return lax.dot_general(x, w, (((1,), (0,)), ((), ())), preferred_element_type=F32)


def table(rows, base, count):
    node = lax.broadcasted_iota(jnp.int32, (count, rows.shape[1]), 0) + base
    return jnp.where(node == rows, 1.0, 0.0).astype(BF16)


def split_bf16(x):
    high = x.astype(BF16)
    return high, (x - high.astype(F32)).astype(BF16)


def kernel(
    groups,
    depth,
    patches,
    control_h,
    members_h,
    conv_h,
    interp_h,
    source_h,
    right_h,
    left_h,
    cells_h,
    weights_h,
    precision_h,
    count_h,
    product_v,
    inc_v,
    control_v,
    members_v,
    conv_v,
    interp_v,
    source_s,
    right_v,
    left_v,
    cells_v,
    weights_v,
    precision_v,
    count_s,
    load_sem,
    right_table,
    left_table,
    halo_send,
    halo_recv,
    halo_send_sem,
    halo_recv_sem,
    edge_acc,
    edge_members,
    conv_f,
    obs_a,
    part,
    arrived,
    part_send_sem,
    part_recv_sem,
    sens,
    sens_send_sem,
    sens_recv_sem,
    nodal,
    give,
    got,
    give_send_sem,
    give_recv_sem,
):
    me = lax.axis_index("member")
    patch = lax.axis_index("patch")
    width = groups // depth
    my_row, my_col = me // depth, lax.rem(me, depth)
    upper, lower = lax.rem(patch + 1, patches), lax.rem(patch + patches - 1, patches)
    mem_here, levels, node_count = control_v.shape
    rows = mem_here * levels
    blocks = node_count // LANES
    edge = 2 * LANES
    factor = 1.0 / math.sqrt(mem_here * groups - 1)
    near = sorted(range(depth), key=lambda d: (min(d, depth - d), d))
    far = near[::-1]

    mirrored = my_row * 2 >= width
    inward = jnp.where(mirrored, width - 1 - my_row, my_row)

    def row_at(turn):
        straight = jnp.where(
            turn < 2, width - 1 - turn, jnp.where(turn == 2, 1 - inward, inward)
        )
        if width < 4:
            straight = lax.rem(my_row + width - 1 - turn, width)
            return straight
        return jnp.where(mirrored, width - 1 - straight, straight)

    def peer(row, step):
        return row * depth + lax.rem(my_col + step, depth)

    def each_far(body):
        lax.fori_loop(0, width, lambda t, carry: (body(row_at(t)), carry)[1], 0)

    def each_near(body, carry=0):
        return lax.fori_loop(0, width, lambda t, c: body(row_at(width - 1 - t), c), carry)

    def unless_me(row, step, act):
        if step == 0:
            pl.when(row != my_row)(act)
        else:
            act()

    barrier = pltpu.get_barrier_semaphore()

    def greet(row):
        for step in far:
            unless_me(
                row,
                step,
                lambda: pl.semaphore_signal(
                    barrier, inc=1, device_id=(peer(row, step), patch), device_id_type=MESH
                ),
            )

    for other in (upper, lower):
        pl.semaphore_signal(barrier, inc=1, device_id=(me, other), device_id_type=MESH)
    each_far(greet)

    sources = (control_h, right_h, left_h, source_h, conv_h, weights_h, precision_h, cells_h, count_h, interp_h, members_h)
    targets = (control_v, right_v, left_v, source_s, conv_v, weights_v, precision_v, cells_v, count_s, interp_v, members_v)
    loads = [
        pltpu.make_async_copy(a, b, load_sem.at[i]) for i, (a, b) in enumerate(zip(sources, targets))
    ]
    for load in loads:
        load.start()

    def node_block(b):
        return control_v[:, :, b * LANES : (b + 1) * LANES].reshape(rows, LANES).astype(BF16)

    for load in loads[:3]:
        load.wait()
    right_table[...] = table(right_v[...], node_count - edge, edge)
    left_table[...] = table(left_v[...], 0, edge)
    last = jnp.concatenate([node_block(blocks - 2), node_block(blocks - 1)], axis=1)
    first = jnp.concatenate([node_block(0), node_block(1)], axis=1)
    halo_send[0] = dot_nn(last, right_table[...]).astype(BF16)
    halo_send[1] = dot_nn(first, left_table[...]).astype(BF16)

    pl.semaphore_wait(barrier, groups + 1)

    def halo_copy(i, other):
        return pltpu.make_async_remote_copy(
            src_ref=halo_send.at[i],
            dst_ref=halo_recv.at[i],
            send_sem=halo_send_sem.at[i],
            recv_sem=halo_recv_sem.at[i],
            device_id=(me, other),
            device_id_type=MESH,
        )

    halos = [halo_copy(0, upper), halo_copy(1, lower)]
    for copy in halos:
        copy.start()

    for load in loads[3:5]:
        load.wait()
    for b in range(blocks):
        acc = dot_nt(node_block(b), conv_v[0, b])
        if b > 0:
            acc = acc + dot_nt(node_block(b - 1), conv_v[1, b])
        if b < blocks - 1:
            acc = acc + dot_nt(node_block(b + 1), conv_v[2, b])
        if b == 0:
            edge_acc[0] = acc
        elif b == blocks - 1:
            edge_acc[1] = acc
        else:
            conv_f[b] = acc.astype(BF16).astype(F32)

    for load in loads[5:9]:
        load.wait()
    slots = cells_v.shape[1]
    own = 2 * LANES
    live = lax.broadcasted_iota(jnp.int32, (1, slots), 1) < count_s[0, 0]
    scaled = jnp.where(live, precision_v[...], 0.0)
    level_w = weights_v[0]
    outer = jnp.concatenate(
        [level_w * (level_w[l : l + 1] * scaled) for l in range(levels)], axis=0
    )
    place = table(cells_v[...], 0, own)
    high, low = split_bf16(outer)
    obs_a[...] = dot_nt(high, place) + dot_nt(low, place)

    for load in loads[9:]:
        load.wait()

    def members_at(c):
        here = members_v[:, :, pl.ds(pl.multiple_of(c * LANES, LANES), LANES)]
        return here.astype(F32)

    def mark_edges(m, carry):
        for h in range(2):
            c = m * 2 + h
            scaled_members = members_at(c) * factor
            at = jnp.full(scaled_members.shape, source_s[c], jnp.int32)
            marked = jnp.stack(
                [jnp.where(at == b, scaled_members, 0.0) for b in (0, blocks - 1)]
            )
            edge_members[m, h] = marked.reshape(2 * mem_here, levels, LANES)
        return carry

    lax.fori_loop(0, groups, mark_edges, 0)

    for copy in halos:
        copy.wait_recv()
    conv_f[0] = (edge_acc[0] + dot_nt(halo_recv[0], conv_v[1, 0])).astype(BF16).astype(F32)
    conv_f[blocks - 1] = (
        (edge_acc[1] + dot_nt(halo_recv[1], conv_v[2, blocks - 1])).astype(BF16).astype(F32)
    )

    def part_copy(m, landing):
        return pltpu.make_async_remote_copy(
            src_ref=part.at[m],
            dst_ref=arrived.at[landing],
            send_sem=part_send_sem.at[m],
            recv_sem=part_recv_sem.at[landing],
            device_id=(m, patch),
            device_id_type=MESH,
        )

    def both(first, second):
        none = jnp.zeros_like(first)
        upper_rows = jnp.concatenate([first, none], axis=1)
        return jnp.concatenate(
            [upper_rows, jnp.concatenate([none, second], axis=1)], axis=0
        ).astype(BF16)

    def forward(row):
        for step in far:
            m = peer(row, step)
            c = m * 2
            picked = both(conv_f[source_s[c]], conv_f[source_s[c + 1]])
            weights = jnp.concatenate([interp_v[c], interp_v[c + 1]], axis=1)
            field = dot_nt(picked, weights).reshape(2, mem_here, levels, LANES)
            perturb = jnp.stack([members_at(c), members_at(c + 1)])
            inc_part = jnp.sum(field * perturb, axis=1)
            part[m] = inc_part.reshape(2 * levels, LANES).astype(BF16)
        for step in far:
            unless_me(row, step, lambda: part_copy(peer(row, step), me).start())

    each_far(forward)

    arrived[me] = part[me]

    def take_in(row, total):
        for step in near:
            m = peer(row, step)
            unless_me(row, step, lambda: part_copy(m, m).wait_recv())
            total = total + arrived[m].astype(F32)
        return total

    total = each_near(take_in, jnp.zeros((2 * levels, LANES), F32))
    inc = total * factor

    pieces = []
    for h in range(2):
        half = inc[h * levels : (h + 1) * levels]
        inc_v[:, h * LANES : (h + 1) * LANES] = half
        acc = None
        for l in range(levels):
            term = (
                obs_a[l * levels : (l + 1) * levels, h * LANES : (h + 1) * LANES]
                * half[l : l + 1]
            )
            acc = term if acc is None else acc + term
        pieces.append(acc)
    sens[me] = jnp.concatenate(pieces, axis=0).astype(BF16)

    def sens_copy(m, landing):
        return pltpu.make_async_remote_copy(
            src_ref=sens.at[landing],
            dst_ref=sens.at[landing],
            send_sem=sens_send_sem.at[m],
            recv_sem=sens_recv_sem.at[landing],
            device_id=(m, patch),
            device_id_type=MESH,
        )

    def share(row):
        for step in far:
            unless_me(row, step, lambda: sens_copy(peer(row, step), me).start())

    each_far(share)

    def weights_of(m):
        return jnp.concatenate([interp_v[m * 2], interp_v[m * 2 + 1]], axis=0)

    def edges(row, total):
        for step in near:
            m = peer(row, step)
            unless_me(row, step, lambda: sens_copy(m, m).wait_recv())
            there = sens[m].astype(F32)
            marked = jnp.concatenate(
                [
                    (edge_members[m, h] * there[h * levels : (h + 1) * levels][None]).reshape(
                        2 * rows, LANES
                    )
                    for h in range(2)
                ],
                axis=1,
            )
            total = total + dot_nn(marked.astype(BF16), weights_of(m))
        return total

    ends = each_near(edges, jnp.zeros((2 * rows, LANES), F32)).astype(BF16)

    def give_copy(i, other):
        return pltpu.make_async_remote_copy(
            src_ref=give.at[i],
            dst_ref=got.at[i],
            send_sem=give_send_sem.at[i],
            recv_sem=give_recv_sem.at[i],
            device_id=(me, other),
            device_id_type=MESH,
        )

    give[0] = dot_nn(ends[:rows], conv_v[1, 0]).astype(BF16)
    give[1] = dot_nn(ends[rows:], conv_v[2, blocks - 1]).astype(BF16)
    gifts = [give_copy(0, lower), give_copy(1, upper)]
    for copy in gifts:
        copy.start()

    nodal[...] = jnp.zeros_like(nodal)
    nodal[0] = ends[:rows].astype(F32)
    nodal[blocks - 1] = ends[rows:].astype(F32)

    chunk = min(groups, 8)

    def backward(turn, carry):
        for pair in range(0, chunk, 2):
            spread = []
            for k in range(2):
                m = turn * chunk + pair + k
                there = sens[m].astype(F32) * factor
                adjoint = [
                    (members_at(m * 2 + h) * there[h * levels : (h + 1) * levels][None]).reshape(
                        rows, LANES
                    )
                    for h in range(2)
                ]
                value = dot_nn(both(*adjoint), weights_of(m))
                for h in range(2):
                    at = jnp.full((rows, LANES), source_s[m * 2 + h], jnp.int32)
                    spread.append((at, value[h * rows : (h + 1) * rows]))
            for b in range(1, blocks - 1):
                acc = nodal[b]
                for at, value in spread:
                    acc = acc + jnp.where(at == b, value, 0.0)
                nodal[b] = acc
        return carry

    lax.fori_loop(0, groups // chunk, backward, 0)

    def node_adjoint(b):
        return nodal[b].astype(BF16)

    for b in range(blocks):
        acc = dot_nn(node_adjoint(b), conv_v[0, b])
        if b < blocks - 1:
            acc = acc + dot_nn(node_adjoint(b + 1), conv_v[1, b + 1])
        if b > 0:
            acc = acc + dot_nn(node_adjoint(b - 1), conv_v[2, b - 1])
        span = slice(b * LANES, (b + 1) * LANES)
        product_v[:, :, span] = control_v[:, :, span] + acc.reshape(mem_here, levels, LANES)

    for i, (tab, start) in enumerate(((right_table, node_count - edge), (left_table, 0))):
        gifts[i].wait_recv()
        added = dot_nt(got[i], tab[...]).reshape(mem_here, levels, edge)
        span = slice(start, start + edge)
        product_v[:, :, span] = product_v[:, :, span] + added

    for copy in halos + gifts:
        copy.wait_send()

    def drain(row):
        for step in near:
            m = peer(row, step)

            def sent():
                part_copy(m, me).wait_send()
                sens_copy(m, me).wait_send()

            unless_me(row, step, sent)

    each_far(drain)


def hand_over(product_v, inc_v, product_h, inc_h, sem):
    outs = [
        pltpu.make_async_copy(product_v, product_h, sem.at[0]),
        pltpu.make_async_copy(inc_v, inc_h, sem.at[1]),
    ]
    for out in outs:
        out.start()
    for out in outs:
        out.wait()


def per_device(*args):
    args = [pltpu.with_memory_space_constraint(a, pltpu.HBM) for a in args[:-1]] + [args[-1]]
    control, members, conv_blocks, interp = args[:4]
    groups, patches = lax.axis_size("member"), lax.axis_size("patch")
    depth = 8 if groups % 8 == 0 else 2
    mem_here, levels, node_count = control.shape
    rows = mem_here * levels
    blocks = node_count // LANES
    slots = args[7].shape[1]
    own = 2 * LANES
    smem = (4, 10)
    loaded = [
        (pltpu.SMEM if i in smem else pltpu.VMEM)(a.shape, a.dtype) for i, a in enumerate(args)
    ]
    dma = pltpu.SemaphoreType.DMA
    piece = (groups, 2 * levels, LANES)
    out_shape = (
        jax.ShapeDtypeStruct(control.shape, F32),
        jax.ShapeDtypeStruct((levels, own), F32),
    )
    results = pl.pallas_call(
        functools.partial(kernel, groups, depth, patches),
        out_shape=tuple(pltpu.VMEM(a.shape, a.dtype) for a in out_shape),
        in_specs=[pl.BlockSpec(memory_space=pltpu.HBM)] * len(args),
        out_specs=[pl.BlockSpec(memory_space=pltpu.VMEM)] * 2,
        scratch_shapes=loaded
        + [
            dma((len(args),)),
            pltpu.VMEM((own, LANES), BF16),
            pltpu.VMEM((own, LANES), BF16),
            pltpu.VMEM((2, rows, LANES), BF16),
            pltpu.VMEM((2, rows, LANES), BF16),
            dma((2,)),
            dma((2,)),
            pltpu.VMEM((2, rows, LANES), F32),
            pltpu.VMEM((groups, 2, 2 * mem_here, levels, LANES), F32),
            pltpu.VMEM((blocks, rows, LANES), F32),
            pltpu.VMEM((levels * levels, own), F32),
            pltpu.VMEM(piece, BF16),
            pltpu.VMEM(piece, BF16),
            dma((groups,)),
            dma((groups,)),
            pltpu.VMEM(piece, BF16),
            dma((groups,)),
            dma((groups,)),
            pltpu.VMEM((blocks, rows, LANES), F32),
            pltpu.VMEM((2, rows, LANES), BF16),
            pltpu.VMEM((2, rows, LANES), BF16),
            dma((2,)),
            dma((2,)),
        ],
        compiler_params=pltpu.CompilerParams(
            collective_id=0, has_side_effects=True, vmem_limit_bytes=VMEM_GRANT
        ),
        name="hessian_step",
    )(*args)
    return pl.pallas_call(
        hand_over,
        out_shape=out_shape,
        in_specs=[pl.BlockSpec(memory_space=pltpu.VMEM)] * 2,
        out_specs=[pl.BlockSpec(memory_space=pl.ANY)] * 2,
        scratch_shapes=[dma((2,))],
        compiler_params=pltpu.CompilerParams(vmem_limit_bytes=VMEM_GRANT),
        name="hand_over",
    )(*results)


def solution(mesh):
    placed = (
        P("member", None, "patch"),
        P("member", None, "patch"),
        P(None, "patch", None, None),
        P("patch", None, None),
        P("patch"),
        P("patch", None),
        P("patch", None),
        P("patch", "member"),
        P("patch", None, "member"),
        P("patch", "member"),
        P("patch", "member"),
    )
    return jax.shard_map(
        per_device,
        mesh=mesh,
        in_specs=placed,
        out_specs=(P("member", None, "patch"), P(None, ("patch", "member"))),
        check_vma=False,
    )
```

```python
import functools
import math

import jax
import jax.numpy as jnp
from jax import lax
from jax.experimental import pallas as pl
from jax.experimental.pallas import tpu as pltpu
from jax.sharding import PartitionSpec as P

F32 = jnp.float32
BF16 = jnp.bfloat16
LANES = 128
VMEM_GRANT = 48 << 20
MESH = pl.DeviceIdType.MESH


def dot_nt(x, w):
    return lax.dot_general(x, w, (((1,), (1,)), ((), ())), preferred_element_type=F32)


def dot_nn(x, w):
    return lax.dot_general(x, w, (((1,), (0,)), ((), ())), preferred_element_type=F32)


def table(rows, base, count):
    node = lax.broadcasted_iota(jnp.int32, (count, rows.shape[1]), 0) + base
    return jnp.where(node == rows, 1.0, 0.0).astype(BF16)


def split_bf16(x):
    high = x.astype(BF16)
    return high, (x - high.astype(F32)).astype(BF16)


def kernel(
    groups,
    depth,
    patches,
    control_h,
    members_h,
    conv_h,
    interp_h,
    source_h,
    right_h,
    left_h,
    cells_h,
    weights_h,
    precision_h,
    count_h,
    product_v,
    inc_v,
    control_v,
    members_v,
    conv_v,
    interp_v,
    source_s,
    right_v,
    left_v,
    cells_v,
    weights_v,
    precision_v,
    count_s,
    load_sem,
    row_sem,
    right_table,
    left_table,
    halo_send,
    halo_recv,
    halo_send_sem,
    halo_recv_sem,
    edge_acc,
    edge_members,
    conv_f,
    obs_a,
    part,
    arrived,
    part_send_sem,
    part_recv_sem,
    sens,
    sens_send_sem,
    sens_recv_sem,
    nodal,
    give,
    got,
    give_send_sem,
    give_recv_sem,
):
    me = lax.axis_index("member")
    patch = lax.axis_index("patch")
    width = groups // depth
    my_row, my_col = me // depth, lax.rem(me, depth)
    upper, lower = lax.rem(patch + 1, patches), lax.rem(patch + patches - 1, patches)
    mem_here, levels, node_count = control_v.shape
    rows = mem_here * levels
    blocks = node_count // LANES
    edge = 2 * LANES
    factor = 1.0 / math.sqrt(mem_here * groups - 1)
    near = sorted(range(depth), key=lambda d: (min(d, depth - d), d))
    far = near[::-1]

    mirrored = my_row * 2 >= width
    inward = jnp.where(mirrored, width - 1 - my_row, my_row)

    def row_at(turn):
        straight = jnp.where(
            turn < 2, width - 1 - turn, jnp.where(turn == 2, 1 - inward, inward)
        )
        if width < 4:
            straight = lax.rem(my_row + width - 1 - turn, width)
            return straight
        return jnp.where(mirrored, width - 1 - straight, straight)

    def peer(row, step):
        return row * depth + lax.rem(my_col + step, depth)

    def each_far(body):
        lax.fori_loop(0, width, lambda t, carry: (body(row_at(t)), carry)[1], 0)

    def each_near(body, carry=0):
        return lax.fori_loop(0, width, lambda t, c: body(row_at(width - 1 - t), c), carry)

    def unless_me(row, step, act):
        if step == 0:
            pl.when(row != my_row)(act)
        else:
            act()

    barrier = pltpu.get_barrier_semaphore()

    def across(turn):
        return lax.rem(my_row + turn, width) * depth + my_col

    def greet(semaphore, m):
        pl.semaphore_signal(semaphore, inc=1, device_id=(m, patch), device_id_type=MESH)

    for other in (upper, lower):
        pl.semaphore_signal(barrier, inc=1, device_id=(me, other), device_id_type=MESH)
    for step in far[:-1]:
        greet(barrier, peer(my_row, step))
    for turn in range(1, width):
        greet(barrier, across(turn))

    sources = (control_h, right_h, left_h, source_h, conv_h, weights_h, precision_h, cells_h, count_h, interp_h, members_h)
    targets = (control_v, right_v, left_v, source_s, conv_v, weights_v, precision_v, cells_v, count_s, interp_v, members_v)
    loads = [
        pltpu.make_async_copy(a, b, load_sem.at[i]) for i, (a, b) in enumerate(zip(sources, targets))
    ]
    for load in loads:
        load.start()

    def node_block(b):
        return control_v[:, :, b * LANES : (b + 1) * LANES].reshape(rows, LANES).astype(BF16)

    for load in loads[:3]:
        load.wait()
    right_table[...] = table(right_v[...], node_count - edge, edge)
    left_table[...] = table(left_v[...], 0, edge)
    last = jnp.concatenate([node_block(blocks - 2), node_block(blocks - 1)], axis=1)
    first = jnp.concatenate([node_block(0), node_block(1)], axis=1)
    halo_send[0] = dot_nn(last, right_table[...]).astype(BF16)
    halo_send[1] = dot_nn(first, left_table[...]).astype(BF16)

    pl.semaphore_wait(barrier, depth + width)

    def halo_copy(i, other):
        return pltpu.make_async_remote_copy(
            src_ref=halo_send.at[i],
            dst_ref=halo_recv.at[i],
            send_sem=halo_send_sem.at[i],
            recv_sem=halo_recv_sem.at[i],
            device_id=(me, other),
            device_id_type=MESH,
        )

    halos = [halo_copy(0, upper), halo_copy(1, lower)]
    for copy in halos:
        copy.start()
    for turn in range(1, width):
        greet(row_sem, across(turn))

    for load in loads[3:5]:
        load.wait()
    for b in range(blocks):
        acc = dot_nt(node_block(b), conv_v[0, b])
        if b > 0:
            acc = acc + dot_nt(node_block(b - 1), conv_v[1, b])
        if b < blocks - 1:
            acc = acc + dot_nt(node_block(b + 1), conv_v[2, b])
        if b == 0:
            edge_acc[0] = acc
        elif b == blocks - 1:
            edge_acc[1] = acc
        else:
            conv_f[b] = acc.astype(BF16).astype(F32)

    for load in loads[5:9]:
        load.wait()
    slots = cells_v.shape[1]
    own = 2 * LANES
    live = lax.broadcasted_iota(jnp.int32, (1, slots), 1) < count_s[0, 0]
    scaled = jnp.where(live, precision_v[...], 0.0)
    level_w = weights_v[0]
    outer = jnp.concatenate(
        [level_w * (level_w[l : l + 1] * scaled) for l in range(levels)], axis=0
    )
    place = table(cells_v[...], 0, own)
    high, low = split_bf16(outer)
    obs_a[...] = dot_nt(high, place) + dot_nt(low, place)

    for load in loads[9:]:
        load.wait()

    def members_at(c):
        here = members_v[:, :, pl.ds(pl.multiple_of(c * LANES, LANES), LANES)]
        return here.astype(F32)

    def mark_edges(m, carry):
        for h in range(2):
            c = m * 2 + h
            scaled_members = members_at(c) * factor
            at = jnp.full(scaled_members.shape, source_s[c], jnp.int32)
            marked = jnp.stack(
                [jnp.where(at == b, scaled_members, 0.0) for b in (0, blocks - 1)]
            )
            edge_members[m, h] = marked.reshape(2 * mem_here, levels, LANES)
        return carry

    lax.fori_loop(0, groups, mark_edges, 0)

    for copy in halos:
        copy.wait_recv()
    conv_f[0] = (edge_acc[0] + dot_nt(halo_recv[0], conv_v[1, 0])).astype(BF16).astype(F32)
    conv_f[blocks - 1] = (
        (edge_acc[1] + dot_nt(halo_recv[1], conv_v[2, blocks - 1])).astype(BF16).astype(F32)
    )

    def part_copy(m, landing):
        return pltpu.make_async_remote_copy(
            src_ref=part.at[m],
            dst_ref=arrived.at[landing],
            send_sem=part_send_sem.at[m],
            recv_sem=part_recv_sem.at[landing],
            device_id=(m, patch),
            device_id_type=MESH,
        )

    def both(first, second):
        none = jnp.zeros_like(first)
        upper_rows = jnp.concatenate([first, none], axis=1)
        return jnp.concatenate(
            [upper_rows, jnp.concatenate([none, second], axis=1)], axis=0
        ).astype(BF16)

    def forward(row):
        for step in far:
            m = peer(row, step)
            c = m * 2
            picked = both(conv_f[source_s[c]], conv_f[source_s[c + 1]])
            weights = jnp.concatenate([interp_v[c], interp_v[c + 1]], axis=1)
            field = dot_nt(picked, weights).reshape(2, mem_here, levels, LANES)
            perturb = jnp.stack([members_at(c), members_at(c + 1)])
            inc_part = jnp.sum(field * perturb, axis=1)
            part[m] = inc_part.reshape(2 * levels, LANES).astype(BF16)
        for step in far:
            unless_me(row, step, lambda: part_copy(peer(row, step), me).start())

    pl.semaphore_wait(row_sem, width - 1)
    each_far(forward)

    arrived[me] = part[me]

    def take_in(row, total):
        for step in near:
            m = peer(row, step)
            unless_me(row, step, lambda: part_copy(m, m).wait_recv())
            total = total + arrived[m].astype(F32)
        return total

    total = each_near(take_in, jnp.zeros((2 * levels, LANES), F32))
    inc = total * factor

    pieces = []
    for h in range(2):
        half = inc[h * levels : (h + 1) * levels]
        inc_v[:, h * LANES : (h + 1) * LANES] = half
        acc = None
        for l in range(levels):
            term = (
                obs_a[l * levels : (l + 1) * levels, h * LANES : (h + 1) * LANES]
                * half[l : l + 1]
            )
            acc = term if acc is None else acc + term
        pieces.append(acc)
    sens[me] = jnp.concatenate(pieces, axis=0).astype(BF16)

    def sens_copy(m, landing):
        return pltpu.make_async_remote_copy(
            src_ref=sens.at[landing],
            dst_ref=sens.at[landing],
            send_sem=sens_send_sem.at[m],
            recv_sem=sens_recv_sem.at[landing],
            device_id=(m, patch),
            device_id_type=MESH,
        )

    def share(row):
        for step in far:
            unless_me(row, step, lambda: sens_copy(peer(row, step), me).start())

    each_far(share)

    def weights_of(m):
        return jnp.concatenate([interp_v[m * 2], interp_v[m * 2 + 1]], axis=0)

    def edges(row, total):
        for step in near:
            m = peer(row, step)
            unless_me(row, step, lambda: sens_copy(m, m).wait_recv())
            there = sens[m].astype(F32)
            marked = jnp.concatenate(
                [
                    (edge_members[m, h] * there[h * levels : (h + 1) * levels][None]).reshape(
                        2 * rows, LANES
                    )
                    for h in range(2)
                ],
                axis=1,
            )
            total = total + dot_nn(marked.astype(BF16), weights_of(m))
        return total

    ends = each_near(edges, jnp.zeros((2 * rows, LANES), F32)).astype(BF16)

    def give_copy(i, other):
        return pltpu.make_async_remote_copy(
            src_ref=give.at[i],
            dst_ref=got.at[i],
            send_sem=give_send_sem.at[i],
            recv_sem=give_recv_sem.at[i],
            device_id=(me, other),
            device_id_type=MESH,
        )

    give[0] = dot_nn(ends[:rows], conv_v[1, 0]).astype(BF16)
    give[1] = dot_nn(ends[rows:], conv_v[2, blocks - 1]).astype(BF16)
    gifts = [give_copy(0, lower), give_copy(1, upper)]
    for copy in gifts:
        copy.start()

    nodal[...] = jnp.zeros_like(nodal)
    nodal[0] = ends[:rows].astype(F32)
    nodal[blocks - 1] = ends[rows:].astype(F32)

    chunk = min(groups, 8)

    def backward(turn, carry):
        for pair in range(0, chunk, 2):
            spread = []
            for k in range(2):
                m = turn * chunk + pair + k
                there = sens[m].astype(F32) * factor
                adjoint = [
                    (members_at(m * 2 + h) * there[h * levels : (h + 1) * levels][None]).reshape(
                        rows, LANES
                    )
                    for h in range(2)
                ]
                value = dot_nn(both(*adjoint), weights_of(m))
                for h in range(2):
                    at = jnp.full((rows, LANES), source_s[m * 2 + h], jnp.int32)
                    spread.append((at, value[h * rows : (h + 1) * rows]))
            for b in range(1, blocks - 1):
                acc = nodal[b]
                for at, value in spread:
                    acc = acc + jnp.where(at == b, value, 0.0)
                nodal[b] = acc
        return carry

    lax.fori_loop(0, groups // chunk, backward, 0)

    def node_adjoint(b):
        return nodal[b].astype(BF16)

    for b in range(blocks):
        acc = dot_nn(node_adjoint(b), conv_v[0, b])
        if b < blocks - 1:
            acc = acc + dot_nn(node_adjoint(b + 1), conv_v[1, b + 1])
        if b > 0:
            acc = acc + dot_nn(node_adjoint(b - 1), conv_v[2, b - 1])
        span = slice(b * LANES, (b + 1) * LANES)
        product_v[:, :, span] = control_v[:, :, span] + acc.reshape(mem_here, levels, LANES)

    def drain(row):
        for step in near:
            m = peer(row, step)

            def sent():
                part_copy(m, me).wait_send()
                sens_copy(m, me).wait_send()

            unless_me(row, step, sent)

    each_far(drain)

    for i, (tab, start) in enumerate(((right_table, node_count - edge), (left_table, 0))):
        gifts[i].wait_recv()
        added = dot_nt(got[i], tab[...]).reshape(mem_here, levels, edge)
        span = slice(start, start + edge)
        product_v[:, :, span] = product_v[:, :, span] + added

    for copy in halos + gifts:
        copy.wait_send()


def hand_over(product_v, inc_v, product_h, inc_h, sem):
    outs = [
        pltpu.make_async_copy(product_v, product_h, sem.at[0]),
        pltpu.make_async_copy(inc_v, inc_h, sem.at[1]),
    ]
    for out in outs:
        out.start()
    for out in outs:
        out.wait()


def per_device(*args):
    args = [pltpu.with_memory_space_constraint(a, pltpu.HBM) for a in args[:-1]] + [args[-1]]
    control, members, conv_blocks, interp = args[:4]
    groups, patches = lax.axis_size("member"), lax.axis_size("patch")
    depth = 8 if groups % 8 == 0 else 2
    mem_here, levels, node_count = control.shape
    rows = mem_here * levels
    blocks = node_count // LANES
    slots = args[7].shape[1]
    own = 2 * LANES
    smem = (4, 10)
    loaded = [
        (pltpu.SMEM if i in smem else pltpu.VMEM)(a.shape, a.dtype) for i, a in enumerate(args)
    ]
    dma = pltpu.SemaphoreType.DMA
    piece = (groups, 2 * levels, LANES)
    out_shape = (
        jax.ShapeDtypeStruct(control.shape, F32),
        jax.ShapeDtypeStruct((levels, own), F32),
    )
    results = pl.pallas_call(
        functools.partial(kernel, groups, depth, patches),
        out_shape=tuple(pltpu.VMEM(a.shape, a.dtype) for a in out_shape),
        in_specs=[pl.BlockSpec(memory_space=pltpu.HBM)] * len(args),
        out_specs=[pl.BlockSpec(memory_space=pltpu.VMEM)] * 2,
        scratch_shapes=loaded
        + [
            dma((len(args),)),
            pltpu.SemaphoreType.REGULAR,
            pltpu.VMEM((own, LANES), BF16),
            pltpu.VMEM((own, LANES), BF16),
            pltpu.VMEM((2, rows, LANES), BF16),
            pltpu.VMEM((2, rows, LANES), BF16),
            dma((2,)),
            dma((2,)),
            pltpu.VMEM((2, rows, LANES), F32),
            pltpu.VMEM((groups, 2, 2 * mem_here, levels, LANES), F32),
            pltpu.VMEM((blocks, rows, LANES), F32),
            pltpu.VMEM((levels * levels, own), F32),
            pltpu.VMEM(piece, BF16),
            pltpu.VMEM(piece, BF16),
            dma((groups,)),
            dma((groups,)),
            pltpu.VMEM(piece, BF16),
            dma((groups,)),
            dma((groups,)),
            pltpu.VMEM((blocks, rows, LANES), F32),
            pltpu.VMEM((2, rows, LANES), BF16),
            pltpu.VMEM((2, rows, LANES), BF16),
            dma((2,)),
            dma((2,)),
        ],
        compiler_params=pltpu.CompilerParams(
            collective_id=0, has_side_effects=True, vmem_limit_bytes=VMEM_GRANT
        ),
        name="hessian_step",
    )(*args)
    return pl.pallas_call(
        hand_over,
        out_shape=out_shape,
        in_specs=[pl.BlockSpec(memory_space=pltpu.VMEM)] * 2,
        out_specs=[pl.BlockSpec(memory_space=pl.ANY)] * 2,
        scratch_shapes=[dma((2,))],
        compiler_params=pltpu.CompilerParams(vmem_limit_bytes=VMEM_GRANT),
        name="hand_over",
    )(*results)


def solution(mesh):
    placed = (
        P("member", None, "patch"),
        P("member", None, "patch"),
        P(None, "patch", None, None),
        P("patch", None, None),
        P("patch"),
        P("patch", None),
        P("patch", None),
        P("patch", "member"),
        P("patch", None, "member"),
        P("patch", "member"),
        P("patch", "member"),
    )
    return jax.shard_map(
        per_device,
        mesh=mesh,
        in_specs=placed,
        out_specs=(P("member", None, "patch"), P(None, ("patch", "member"))),
        check_vma=False,
    )
```

```python
import functools
import math

import jax
import jax.numpy as jnp
from jax import lax
from jax.experimental import pallas as pl
from jax.experimental.pallas import tpu as pltpu
from jax.sharding import PartitionSpec as P

F32 = jnp.float32
BF16 = jnp.bfloat16
LANES = 128
VMEM_GRANT = 48 << 20
MESH = pl.DeviceIdType.MESH


def dot_nt(x, w):
    return lax.dot_general(x, w, (((1,), (1,)), ((), ())), preferred_element_type=F32)


def dot_nn(x, w):
    return lax.dot_general(x, w, (((1,), (0,)), ((), ())), preferred_element_type=F32)


def table(rows, base, count):
    node = lax.broadcasted_iota(jnp.int32, (count, rows.shape[1]), 0) + base
    return jnp.where(node == rows, 1.0, 0.0).astype(BF16)


def split_bf16(x):
    high = x.astype(BF16)
    return high, (x - high.astype(F32)).astype(BF16)


def kernel(
    groups,
    depth,
    patches,
    control_h,
    members_h,
    conv_h,
    interp_h,
    source_h,
    right_h,
    left_h,
    cells_h,
    weights_h,
    precision_h,
    count_h,
    product_v,
    inc_v,
    control_v,
    members_v,
    conv_v,
    interp_v,
    source_s,
    right_v,
    left_v,
    cells_v,
    weights_v,
    precision_v,
    count_s,
    load_sem,
    row_sem,
    right_table,
    left_table,
    halo_send,
    halo_recv,
    halo_send_sem,
    halo_recv_sem,
    edge_acc,
    edge_members,
    conv_f,
    obs_a,
    part,
    arrived,
    part_send_sem,
    part_recv_sem,
    sens,
    sens_send_sem,
    sens_recv_sem,
    nodal,
    give,
    got,
    give_send_sem,
    give_recv_sem,
):
    me = lax.axis_index("member")
    patch = lax.axis_index("patch")
    width = groups // depth
    my_row, my_col = me // depth, lax.rem(me, depth)
    upper, lower = lax.rem(patch + 1, patches), lax.rem(patch + patches - 1, patches)
    mem_here, levels, node_count = control_v.shape
    rows = mem_here * levels
    blocks = node_count // LANES
    edge = 2 * LANES
    factor = 1.0 / math.sqrt(mem_here * groups - 1)
    near = sorted(range(depth), key=lambda d: (min(d, depth - d), d))
    far = near[::-1]

    mirrored = my_row * 2 >= width
    inward = jnp.where(mirrored, width - 1 - my_row, my_row)

    def row_at(turn):
        straight = jnp.where(
            turn < 2, width - 1 - turn, jnp.where(turn == 2, 1 - inward, inward)
        )
        if width < 4:
            straight = lax.rem(my_row + width - 1 - turn, width)
            return straight
        return jnp.where(mirrored, width - 1 - straight, straight)

    def peer(row, step):
        return row * depth + lax.rem(my_col + step, depth)

    def each_far(body):
        lax.fori_loop(0, width, lambda t, carry: (body(row_at(t)), carry)[1], 0)

    def each_near(body, carry=0):
        return lax.fori_loop(0, width, lambda t, c: body(row_at(width - 1 - t), c), carry)

    def unless_me(row, step, act):
        if step == 0:
            pl.when(row != my_row)(act)
        else:
            act()

    barrier = pltpu.get_barrier_semaphore()

    def across(turn):
        return lax.rem(my_row + turn, width) * depth + my_col

    def greet(semaphore, m):
        pl.semaphore_signal(semaphore, inc=1, device_id=(m, patch), device_id_type=MESH)

    for other in (upper, lower):
        pl.semaphore_signal(barrier, inc=1, device_id=(me, other), device_id_type=MESH)
    for step in far[:-1]:
        greet(barrier, peer(my_row, step))
    for turn in range(1, width):
        greet(barrier, across(turn))

    sources = (control_h, right_h, left_h, source_h, conv_h, weights_h, precision_h, cells_h, count_h, interp_h, members_h)
    targets = (control_v, right_v, left_v, source_s, conv_v, weights_v, precision_v, cells_v, count_s, interp_v, members_v)
    loads = [
        pltpu.make_async_copy(a, b, load_sem.at[i]) for i, (a, b) in enumerate(zip(sources, targets))
    ]
    for load in loads:
        load.start()

    def node_block(b):
        return control_v[:, :, b * LANES : (b + 1) * LANES].reshape(rows, LANES).astype(BF16)

    for load in loads[:3]:
        load.wait()
    right_table[...] = table(right_v[...], node_count - edge, edge)
    left_table[...] = table(left_v[...], 0, edge)
    last = jnp.concatenate([node_block(blocks - 2), node_block(blocks - 1)], axis=1)
    first = jnp.concatenate([node_block(0), node_block(1)], axis=1)
    halo_send[0] = dot_nn(last, right_table[...]).astype(BF16)
    halo_send[1] = dot_nn(first, left_table[...]).astype(BF16)

    pl.semaphore_wait(barrier, depth + width)

    def halo_copy(i, other):
        return pltpu.make_async_remote_copy(
            src_ref=halo_send.at[i],
            dst_ref=halo_recv.at[i],
            send_sem=halo_send_sem.at[i],
            recv_sem=halo_recv_sem.at[i],
            device_id=(me, other),
            device_id_type=MESH,
        )

    halos = [halo_copy(0, upper), halo_copy(1, lower)]
    for copy in halos:
        copy.start()
    for turn in range(1, width):
        greet(row_sem, across(turn))

    for load in loads[3:5]:
        load.wait()
    for b in range(blocks):
        acc = dot_nt(node_block(b), conv_v[0, b])
        if b > 0:
            acc = acc + dot_nt(node_block(b - 1), conv_v[1, b])
        if b < blocks - 1:
            acc = acc + dot_nt(node_block(b + 1), conv_v[2, b])
        if b == 0:
            edge_acc[0] = acc
        elif b == blocks - 1:
            edge_acc[1] = acc
        else:
            conv_f[b] = acc.astype(BF16).astype(F32)

    for load in loads[5:9]:
        load.wait()
    slots = cells_v.shape[1]
    own = 2 * LANES
    live = lax.broadcasted_iota(jnp.int32, (1, slots), 1) < count_s[0, 0]
    scaled = jnp.where(live, precision_v[...], 0.0)
    level_w = weights_v[0]
    outer = jnp.concatenate(
        [level_w * (level_w[l : l + 1] * scaled) for l in range(levels)], axis=0
    )
    place = table(cells_v[...], 0, own)
    high, low = split_bf16(outer)
    obs_a[...] = dot_nt(high, place) + dot_nt(low, place)

    for load in loads[9:]:
        load.wait()

    def members_at(c):
        here = members_v[:, :, pl.ds(pl.multiple_of(c * LANES, LANES), LANES)]
        return here.astype(F32)

    def mark_edges(m, carry):
        for h in range(2):
            c = m * 2 + h
            scaled_members = members_at(c) * factor
            at = jnp.full(scaled_members.shape, source_s[c], jnp.int32)
            marked = jnp.stack(
                [jnp.where(at == b, scaled_members, 0.0) for b in (0, blocks - 1)]
            )
            edge_members[m, h] = marked.reshape(2 * mem_here, levels, LANES)
        return carry

    lax.fori_loop(0, groups, mark_edges, 0)

    for copy in halos:
        copy.wait_recv()
    conv_f[0] = (edge_acc[0] + dot_nt(halo_recv[0], conv_v[1, 0])).astype(BF16).astype(F32)
    conv_f[blocks - 1] = (
        (edge_acc[1] + dot_nt(halo_recv[1], conv_v[2, blocks - 1])).astype(BF16).astype(F32)
    )

    def part_copy(m, landing):
        return pltpu.make_async_remote_copy(
            src_ref=part.at[m],
            dst_ref=arrived.at[landing],
            send_sem=part_send_sem.at[m],
            recv_sem=part_recv_sem.at[landing],
            device_id=(m, patch),
            device_id_type=MESH,
        )

    def both(first, second):
        none = jnp.zeros_like(first)
        upper_rows = jnp.concatenate([first, none], axis=1)
        return jnp.concatenate(
            [upper_rows, jnp.concatenate([none, second], axis=1)], axis=0
        ).astype(BF16)

    def forward(row):
        for batch in (far[: depth // 2], far[depth // 2 :]):
            for step in batch:
                m = peer(row, step)
                c = m * 2
                picked = both(conv_f[source_s[c]], conv_f[source_s[c + 1]])
                weights = jnp.concatenate([interp_v[c], interp_v[c + 1]], axis=1)
                field = dot_nt(picked, weights).reshape(2, mem_here, levels, LANES)
                perturb = jnp.stack([members_at(c), members_at(c + 1)])
                inc_part = jnp.sum(field * perturb, axis=1)
                part[m] = inc_part.reshape(2 * levels, LANES).astype(BF16)
            for step in batch:
                unless_me(row, step, lambda: part_copy(peer(row, step), me).start())

    pl.semaphore_wait(row_sem, width - 1)
    each_far(forward)

    arrived[me] = part[me]

    def take_in(row, carry):
        for step in near:
            m = peer(row, step)
            unless_me(row, step, lambda: part_copy(m, m).wait_recv())
        return carry

    each_near(take_in)
    sums = [arrived[m].astype(F32) for m in range(groups)]
    while len(sums) > 1:
        sums = [a + b for a, b in zip(sums[::2], sums[1::2])]
    total = sums[0]
    inc = total * factor

    pieces = []
    for h in range(2):
        half = inc[h * levels : (h + 1) * levels]
        inc_v[:, h * LANES : (h + 1) * LANES] = half
        acc = None
        for l in range(levels):
            term = (
                obs_a[l * levels : (l + 1) * levels, h * LANES : (h + 1) * LANES]
                * half[l : l + 1]
            )
            acc = term if acc is None else acc + term
        pieces.append(acc)
    sens[me] = jnp.concatenate(pieces, axis=0).astype(BF16)

    def sens_copy(m, landing):
        return pltpu.make_async_remote_copy(
            src_ref=sens.at[landing],
            dst_ref=sens.at[landing],
            send_sem=sens_send_sem.at[m],
            recv_sem=sens_recv_sem.at[landing],
            device_id=(m, patch),
            device_id_type=MESH,
        )

    def share(row):
        for step in far:
            unless_me(row, step, lambda: sens_copy(peer(row, step), me).start())

    each_far(share)

    def weights_of(m):
        return jnp.concatenate([interp_v[m * 2], interp_v[m * 2 + 1]], axis=0)

    def edges(row, total):
        for pair in range(0, depth, 2):
            peers = [peer(row, step) for step in near[pair : pair + 2]]
            for step, m in zip(near[pair : pair + 2], peers):
                unless_me(row, step, lambda: sens_copy(m, m).wait_recv())
            added = []
            for m in peers:
                there = sens[m].astype(F32)
                marked = jnp.concatenate(
                    [
                        (edge_members[m, h] * there[h * levels : (h + 1) * levels][None]).reshape(
                            2 * rows, LANES
                        )
                        for h in range(2)
                    ],
                    axis=1,
                )
                added.append(dot_nn(marked.astype(BF16), weights_of(m)))
            total = total + (added[0] + added[1])
        return total

    ends = each_near(edges, jnp.zeros((2 * rows, LANES), F32)).astype(BF16)

    def give_copy(i, other):
        return pltpu.make_async_remote_copy(
            src_ref=give.at[i],
            dst_ref=got.at[i],
            send_sem=give_send_sem.at[i],
            recv_sem=give_recv_sem.at[i],
            device_id=(me, other),
            device_id_type=MESH,
        )

    give[0] = dot_nn(ends[:rows], conv_v[1, 0]).astype(BF16)
    give[1] = dot_nn(ends[rows:], conv_v[2, blocks - 1]).astype(BF16)
    gifts = [give_copy(0, lower), give_copy(1, upper)]
    for copy in gifts:
        copy.start()

    nodal[...] = jnp.zeros_like(nodal)
    nodal[0] = ends[:rows].astype(F32)
    nodal[blocks - 1] = ends[rows:].astype(F32)

    chunk = min(groups, 8)

    def backward(turn, carry):
        for pair in range(0, chunk, 2):
            spread = []
            for k in range(2):
                m = turn * chunk + pair + k
                there = sens[m].astype(F32) * factor
                adjoint = [
                    (members_at(m * 2 + h) * there[h * levels : (h + 1) * levels][None]).reshape(
                        rows, LANES
                    )
                    for h in range(2)
                ]
                value = dot_nn(both(*adjoint), weights_of(m))
                for h in range(2):
                    at = jnp.full((rows, LANES), source_s[m * 2 + h], jnp.int32)
                    spread.append((at, value[h * rows : (h + 1) * rows]))
            for b in range(1, blocks - 1):
                acc = nodal[b]
                for at, value in spread:
                    acc = acc + jnp.where(at == b, value, 0.0)
                nodal[b] = acc
        return carry

    lax.fori_loop(0, groups // chunk, backward, 0)

    def node_adjoint(b):
        return nodal[b].astype(BF16)

    for b in range(blocks):
        acc = dot_nn(node_adjoint(b), conv_v[0, b])
        if b < blocks - 1:
            acc = acc + dot_nn(node_adjoint(b + 1), conv_v[1, b + 1])
        if b > 0:
            acc = acc + dot_nn(node_adjoint(b - 1), conv_v[2, b - 1])
        span = slice(b * LANES, (b + 1) * LANES)
        product_v[:, :, span] = control_v[:, :, span] + acc.reshape(mem_here, levels, LANES)

    def drain(row):
        for step in near:
            m = peer(row, step)

            def sent():
                part_copy(m, me).wait_send()
                sens_copy(m, me).wait_send()

            unless_me(row, step, sent)

    each_far(drain)

    for i, (tab, start) in enumerate(((right_table, node_count - edge), (left_table, 0))):
        gifts[i].wait_recv()
        added = dot_nt(got[i], tab[...]).reshape(mem_here, levels, edge)
        span = slice(start, start + edge)
        product_v[:, :, span] = product_v[:, :, span] + added

    for copy in halos + gifts:
        copy.wait_send()


def hand_over(product_v, inc_v, product_h, inc_h, sem):
    outs = [pltpu.make_async_copy(inc_v, inc_h, sem.at[0])]
    for k in range(product_v.shape[0]):
        outs.append(pltpu.make_async_copy(product_v.at[k], product_h.at[k], sem.at[k + 1]))
    for out in outs:
        out.start()
    for out in outs:
        out.wait()


def per_device(*args):
    args = [pltpu.with_memory_space_constraint(a, pltpu.HBM) for a in args[:-1]] + [args[-1]]
    control, members, conv_blocks, interp = args[:4]
    groups, patches = lax.axis_size("member"), lax.axis_size("patch")
    depth = 8 if groups % 8 == 0 else 2
    mem_here, levels, node_count = control.shape
    rows = mem_here * levels
    blocks = node_count // LANES
    slots = args[7].shape[1]
    own = 2 * LANES
    smem = (4, 10)
    loaded = [
        (pltpu.SMEM if i in smem else pltpu.VMEM)(a.shape, a.dtype) for i, a in enumerate(args)
    ]
    dma = pltpu.SemaphoreType.DMA
    piece = (groups, 2 * levels, LANES)
    out_shape = (
        jax.ShapeDtypeStruct(control.shape, F32),
        jax.ShapeDtypeStruct((levels, own), F32),
    )
    results = pl.pallas_call(
        functools.partial(kernel, groups, depth, patches),
        out_shape=tuple(pltpu.VMEM(a.shape, a.dtype) for a in out_shape),
        in_specs=[pl.BlockSpec(memory_space=pltpu.HBM)] * len(args),
        out_specs=[pl.BlockSpec(memory_space=pltpu.VMEM)] * 2,
        scratch_shapes=loaded
        + [
            dma((len(args),)),
            pltpu.SemaphoreType.REGULAR,
            pltpu.VMEM((own, LANES), BF16),
            pltpu.VMEM((own, LANES), BF16),
            pltpu.VMEM((2, rows, LANES), BF16),
            pltpu.VMEM((2, rows, LANES), BF16),
            dma((2,)),
            dma((2,)),
            pltpu.VMEM((2, rows, LANES), F32),
            pltpu.VMEM((groups, 2, 2 * mem_here, levels, LANES), F32),
            pltpu.VMEM((blocks, rows, LANES), F32),
            pltpu.VMEM((levels * levels, own), F32),
            pltpu.VMEM(piece, BF16),
            pltpu.VMEM(piece, BF16),
            dma((groups,)),
            dma((groups,)),
            pltpu.VMEM(piece, BF16),
            dma((groups,)),
            dma((groups,)),
            pltpu.VMEM((blocks, rows, LANES), F32),
            pltpu.VMEM((2, rows, LANES), BF16),
            pltpu.VMEM((2, rows, LANES), BF16),
            dma((2,)),
            dma((2,)),
        ],
        compiler_params=pltpu.CompilerParams(
            collective_id=0, has_side_effects=True, vmem_limit_bytes=VMEM_GRANT
        ),
        name="hessian_step",
    )(*args)
    return pl.pallas_call(
        hand_over,
        out_shape=out_shape,
        in_specs=[pl.BlockSpec(memory_space=pltpu.VMEM)] * 2,
        out_specs=[pl.BlockSpec(memory_space=pl.ANY)] * 2,
        scratch_shapes=[dma((mem_here + 1,))],
        compiler_params=pltpu.CompilerParams(vmem_limit_bytes=VMEM_GRANT),
        name="hand_over",
    )(*results)


def solution(mesh):
    placed = (
        P("member", None, "patch"),
        P("member", None, "patch"),
        P(None, "patch", None, None),
        P("patch", None, None),
        P("patch"),
        P("patch", None),
        P("patch", None),
        P("patch", "member"),
        P("patch", None, "member"),
        P("patch", "member"),
        P("patch", "member"),
    )
    return jax.shard_map(
        per_device,
        mesh=mesh,
        in_specs=placed,
        out_specs=(P("member", None, "patch"), P(None, ("patch", "member"))),
        check_vma=False,
    )
```

```python
import functools
import math

import jax
import jax.numpy as jnp
from jax import lax
from jax.experimental import pallas as pl
from jax.experimental.pallas import tpu as pltpu
from jax.sharding import PartitionSpec as P

F32 = jnp.float32
BF16 = jnp.bfloat16
LANES = 128
VMEM_GRANT = 48 << 20
MESH = pl.DeviceIdType.MESH


def dot_nt(x, w):
    return lax.dot_general(x, w, (((1,), (1,)), ((), ())), preferred_element_type=F32)


def dot_nn(x, w):
    return lax.dot_general(x, w, (((1,), (0,)), ((), ())), preferred_element_type=F32)


def table(rows, base, count):
    node = lax.broadcasted_iota(jnp.int32, (count, rows.shape[1]), 0) + base
    return jnp.where(node == rows, 1.0, 0.0).astype(BF16)


def split_bf16(x):
    high = x.astype(BF16)
    return high, (x - high.astype(F32)).astype(BF16)


def kernel(
    groups,
    depth,
    patches,
    control_h,
    members_h,
    conv_h,
    interp_h,
    source_h,
    right_h,
    left_h,
    cells_h,
    weights_h,
    precision_h,
    count_h,
    product_v,
    inc_v,
    control_v,
    members_v,
    conv_v,
    interp_v,
    source_s,
    right_v,
    left_v,
    cells_v,
    weights_v,
    precision_v,
    count_s,
    load_sem,
    row_sem,
    right_table,
    left_table,
    halo_send,
    halo_recv,
    halo_send_sem,
    halo_recv_sem,
    edge_acc,
    edge_members,
    conv_f,
    obs_a,
    part,
    arrived,
    part_send_sem,
    part_recv_sem,
    sens,
    sens_send_sem,
    sens_recv_sem,
    nodal,
    give,
    got,
    give_send_sem,
    give_recv_sem,
):
    me = lax.axis_index("member")
    patch = lax.axis_index("patch")
    width = groups // depth
    my_row, my_col = me // depth, lax.rem(me, depth)
    upper, lower = lax.rem(patch + 1, patches), lax.rem(patch + patches - 1, patches)
    mem_here, levels, node_count = control_v.shape
    rows = mem_here * levels
    blocks = node_count // LANES
    edge = 2 * LANES
    factor = 1.0 / math.sqrt(mem_here * groups - 1)
    near = sorted(range(depth), key=lambda d: (min(d, depth - d), d))
    far = near[::-1]

    mirrored = my_row * 2 >= width
    inward = jnp.where(mirrored, width - 1 - my_row, my_row)

    def row_at(turn):
        straight = jnp.where(
            turn < 2, width - 1 - turn, jnp.where(turn == 2, 1 - inward, inward)
        )
        if width < 4:
            straight = lax.rem(my_row + width - 1 - turn, width)
            return straight
        return jnp.where(mirrored, width - 1 - straight, straight)

    def peer(row, step):
        return row * depth + lax.rem(my_col + step, depth)

    def each_far(body):
        lax.fori_loop(0, width, lambda t, carry: (body(row_at(t)), carry)[1], 0)

    def each_near(body, carry=0):
        return lax.fori_loop(0, width, lambda t, c: body(row_at(width - 1 - t), c), carry)

    def unless_me(row, step, act):
        if step == 0:
            pl.when(row != my_row)(act)
        else:
            act()

    barrier = pltpu.get_barrier_semaphore()

    def across(turn):
        return lax.rem(my_row + turn, width) * depth + my_col

    def greet(semaphore, m):
        pl.semaphore_signal(semaphore, inc=1, device_id=(m, patch), device_id_type=MESH)

    for other in (upper, lower):
        pl.semaphore_signal(barrier, inc=1, device_id=(me, other), device_id_type=MESH)
    for step in far[:-1]:
        greet(barrier, peer(my_row, step))
    for turn in range(1, width):
        greet(barrier, across(turn))

    sources = (control_h, right_h, left_h, source_h, conv_h, weights_h, precision_h, cells_h, count_h, interp_h, members_h)
    targets = (control_v, right_v, left_v, source_s, conv_v, weights_v, precision_v, cells_v, count_s, interp_v, members_v)
    loads = [
        pltpu.make_async_copy(a, b, load_sem.at[i]) for i, (a, b) in enumerate(zip(sources, targets))
    ]
    for load in loads:
        load.start()

    def node_block(b):
        return control_v[:, :, b * LANES : (b + 1) * LANES].reshape(rows, LANES).astype(BF16)

    for load in loads[:3]:
        load.wait()
    right_table[...] = table(right_v[...], node_count - edge, edge)
    left_table[...] = table(left_v[...], 0, edge)
    last = jnp.concatenate([node_block(blocks - 2), node_block(blocks - 1)], axis=1)
    first = jnp.concatenate([node_block(0), node_block(1)], axis=1)
    halo_send[0] = dot_nn(last, right_table[...]).astype(BF16)
    halo_send[1] = dot_nn(first, left_table[...]).astype(BF16)

    pl.semaphore_wait(barrier, depth + width)

    def halo_copy(i, other):
        return pltpu.make_async_remote_copy(
            src_ref=halo_send.at[i],
            dst_ref=halo_recv.at[i],
            send_sem=halo_send_sem.at[i],
            recv_sem=halo_recv_sem.at[i],
            device_id=(me, other),
            device_id_type=MESH,
        )

    halos = [halo_copy(0, upper), halo_copy(1, lower)]
    for copy in halos:
        copy.start()
    for turn in range(1, width):
        greet(row_sem, across(turn))

    for load in loads[3:5]:
        load.wait()
    for b in range(blocks):
        acc = dot_nt(node_block(b), conv_v[0, b])
        if b > 0:
            acc = acc + dot_nt(node_block(b - 1), conv_v[1, b])
        if b < blocks - 1:
            acc = acc + dot_nt(node_block(b + 1), conv_v[2, b])
        if b == 0:
            edge_acc[0] = acc
        elif b == blocks - 1:
            edge_acc[1] = acc
        else:
            conv_f[b] = acc.astype(BF16).astype(F32)

    for load in loads[5:9]:
        load.wait()
    slots = cells_v.shape[1]
    own = 2 * LANES
    live = lax.broadcasted_iota(jnp.int32, (1, slots), 1) < count_s[0, 0]
    scaled = jnp.where(live, precision_v[...], 0.0)
    level_w = weights_v[0]
    outer = jnp.concatenate(
        [level_w * (level_w[l : l + 1] * scaled) for l in range(levels)], axis=0
    )
    place = table(cells_v[...], 0, own)
    high, low = split_bf16(outer)
    obs_a[...] = dot_nt(high, place) + dot_nt(low, place)

    for load in loads[9:]:
        load.wait()

    def members_at(c):
        here = members_v[:, :, pl.ds(pl.multiple_of(c * LANES, LANES), LANES)]
        return here.astype(F32)

    def mark_edges(m, carry):
        for h in range(2):
            c = m * 2 + h
            scaled_members = members_at(c) * factor
            at = jnp.full(scaled_members.shape, source_s[c], jnp.int32)
            marked = jnp.stack(
                [jnp.where(at == b, scaled_members, 0.0) for b in (0, blocks - 1)]
            )
            edge_members[m, h] = marked.reshape(2 * mem_here, levels, LANES)
        return carry

    lax.fori_loop(0, groups, mark_edges, 0)

    for copy in halos:
        copy.wait_recv()
    conv_f[0] = (edge_acc[0] + dot_nt(halo_recv[0], conv_v[1, 0])).astype(BF16).astype(F32)
    conv_f[blocks - 1] = (
        (edge_acc[1] + dot_nt(halo_recv[1], conv_v[2, blocks - 1])).astype(BF16).astype(F32)
    )

    def part_copy(m, landing):
        return pltpu.make_async_remote_copy(
            src_ref=part.at[m],
            dst_ref=arrived.at[landing],
            send_sem=part_send_sem.at[m],
            recv_sem=part_recv_sem.at[landing],
            device_id=(m, patch),
            device_id_type=MESH,
        )

    def both(first, second):
        none = jnp.zeros_like(first)
        upper_rows = jnp.concatenate([first, none], axis=1)
        return jnp.concatenate(
            [upper_rows, jnp.concatenate([none, second], axis=1)], axis=0
        ).astype(BF16)

    def forward(row):
        for batch in (far[: depth // 2], far[depth // 2 :]):
            for step in batch:
                m = peer(row, step)
                c = m * 2
                picked = both(conv_f[source_s[c]], conv_f[source_s[c + 1]])
                weights = jnp.concatenate([interp_v[c], interp_v[c + 1]], axis=1)
                field = dot_nt(picked, weights).reshape(2, mem_here, levels, LANES)
                perturb = jnp.stack([members_at(c), members_at(c + 1)])
                inc_part = jnp.sum(field * perturb, axis=1)
                part[m] = inc_part.reshape(2 * levels, LANES).astype(BF16)
            for step in batch:
                unless_me(row, step, lambda: part_copy(peer(row, step), me).start())

    pl.semaphore_wait(row_sem, width - 1)
    each_far(forward)

    arrived[me] = part[me]

    def take_in(row, carry):
        for step in near:
            m = peer(row, step)
            unless_me(row, step, lambda: part_copy(m, m).wait_recv())
        return carry

    each_near(take_in)
    sums = [arrived[m].astype(F32) for m in range(groups)]
    while len(sums) > 1:
        sums = [a + b for a, b in zip(sums[::2], sums[1::2])]
    total = sums[0]
    inc = total * factor

    pieces = []
    for h in range(2):
        half = inc[h * levels : (h + 1) * levels]
        inc_v[:, h * LANES : (h + 1) * LANES] = half
        acc = None
        for l in range(levels):
            term = (
                obs_a[l * levels : (l + 1) * levels, h * LANES : (h + 1) * LANES]
                * half[l : l + 1]
            )
            acc = term if acc is None else acc + term
        pieces.append(acc)
    sens[me] = jnp.concatenate(pieces, axis=0).astype(BF16)

    def sens_copy(m, landing):
        return pltpu.make_async_remote_copy(
            src_ref=sens.at[landing],
            dst_ref=sens.at[landing],
            send_sem=sens_send_sem.at[m],
            recv_sem=sens_recv_sem.at[landing],
            device_id=(m, patch),
            device_id_type=MESH,
        )

    def share(row):
        for step in far:
            unless_me(row, step, lambda: sens_copy(peer(row, step), me).start())

    each_far(share)

    def weights_of(m):
        return jnp.concatenate([interp_v[m * 2], interp_v[m * 2 + 1]], axis=0)

    def edges(row, total):
        for pair in range(0, depth, 8):
            peers = [peer(row, step) for step in near[pair : pair + 8]]
            for step, m in zip(near[pair : pair + 8], peers):
                unless_me(row, step, lambda: sens_copy(m, m).wait_recv())
            added = []
            for m in peers:
                there = sens[m].astype(F32)
                marked = jnp.concatenate(
                    [
                        (edge_members[m, h] * there[h * levels : (h + 1) * levels][None]).reshape(
                            2 * rows, LANES
                        )
                        for h in range(2)
                    ],
                    axis=1,
                )
                added.append(dot_nn(marked.astype(BF16), weights_of(m)))
            while len(added) > 1:
                added = [a + b for a, b in zip(added[::2], added[1::2])]
            total = total + added[0]
        return total

    ends = each_near(edges, jnp.zeros((2 * rows, LANES), F32)).astype(BF16)

    def give_copy(i, other):
        return pltpu.make_async_remote_copy(
            src_ref=give.at[i],
            dst_ref=got.at[i],
            send_sem=give_send_sem.at[i],
            recv_sem=give_recv_sem.at[i],
            device_id=(me, other),
            device_id_type=MESH,
        )

    give[0] = dot_nn(ends[:rows], conv_v[1, 0]).astype(BF16)
    give[1] = dot_nn(ends[rows:], conv_v[2, blocks - 1]).astype(BF16)
    gifts = [give_copy(0, lower), give_copy(1, upper)]
    for copy in gifts:
        copy.start()

    nodal[...] = jnp.zeros_like(nodal)
    nodal[0] = ends[:rows].astype(F32)
    nodal[blocks - 1] = ends[rows:].astype(F32)

    chunk = min(groups, 8)

    def backward(turn, carry):
        for pair in range(0, chunk, 2):
            spread = []
            for k in range(2):
                m = turn * chunk + pair + k
                there = sens[m].astype(F32) * factor
                adjoint = [
                    (members_at(m * 2 + h) * there[h * levels : (h + 1) * levels][None]).reshape(
                        rows, LANES
                    )
                    for h in range(2)
                ]
                value = dot_nn(both(*adjoint), weights_of(m))
                for h in range(2):
                    at = jnp.full((rows, LANES), source_s[m * 2 + h], jnp.int32)
                    spread.append((at, value[h * rows : (h + 1) * rows]))
            for b in range(1, blocks - 1):
                acc = nodal[b]
                for at, value in spread:
                    acc = acc + jnp.where(at == b, value, 0.0)
                nodal[b] = acc
        return carry

    lax.fori_loop(0, groups // chunk, backward, 0)

    def node_adjoint(b):
        return nodal[b].astype(BF16)

    for b in range(blocks):
        acc = dot_nn(node_adjoint(b), conv_v[0, b])
        if b < blocks - 1:
            acc = acc + dot_nn(node_adjoint(b + 1), conv_v[1, b + 1])
        if b > 0:
            acc = acc + dot_nn(node_adjoint(b - 1), conv_v[2, b - 1])
        span = slice(b * LANES, (b + 1) * LANES)
        product_v[:, :, span] = control_v[:, :, span] + acc.reshape(mem_here, levels, LANES)

    def drain(row):
        for step in near:
            m = peer(row, step)

            def sent():
                part_copy(m, me).wait_send()
                sens_copy(m, me).wait_send()

            unless_me(row, step, sent)

    each_far(drain)

    for copy in gifts:
        copy.wait_recv()
    for i, (tab, start) in enumerate(((right_table, node_count - edge), (left_table, 0))):
        added = dot_nt(got[i], tab[...]).reshape(mem_here, levels, edge)
        span = slice(start, start + edge)
        product_v[:, :, span] = product_v[:, :, span] + added

    for copy in halos + gifts:
        copy.wait_send()


def hand_over(product_v, inc_v, product_h, inc_h, sem):
    outs = [pltpu.make_async_copy(inc_v, inc_h, sem.at[0])]
    for k in range(product_v.shape[0]):
        outs.append(pltpu.make_async_copy(product_v.at[k], product_h.at[k], sem.at[k + 1]))
    for out in outs:
        out.start()
    for out in outs:
        out.wait()


def per_device(*args):
    args = [pltpu.with_memory_space_constraint(a, pltpu.HBM) for a in args[:-1]] + [args[-1]]
    control, members, conv_blocks, interp = args[:4]
    groups, patches = lax.axis_size("member"), lax.axis_size("patch")
    depth = 8 if groups % 8 == 0 else 2
    mem_here, levels, node_count = control.shape
    rows = mem_here * levels
    blocks = node_count // LANES
    slots = args[7].shape[1]
    own = 2 * LANES
    smem = (4, 10)
    loaded = [
        (pltpu.SMEM if i in smem else pltpu.VMEM)(a.shape, a.dtype) for i, a in enumerate(args)
    ]
    dma = pltpu.SemaphoreType.DMA
    piece = (groups, 2 * levels, LANES)
    out_shape = (
        jax.ShapeDtypeStruct(control.shape, F32),
        jax.ShapeDtypeStruct((levels, own), F32),
    )
    results = pl.pallas_call(
        functools.partial(kernel, groups, depth, patches),
        out_shape=tuple(pltpu.VMEM(a.shape, a.dtype) for a in out_shape),
        in_specs=[pl.BlockSpec(memory_space=pltpu.HBM)] * len(args),
        out_specs=[pl.BlockSpec(memory_space=pltpu.VMEM)] * 2,
        scratch_shapes=loaded
        + [
            dma((len(args),)),
            pltpu.SemaphoreType.REGULAR,
            pltpu.VMEM((own, LANES), BF16),
            pltpu.VMEM((own, LANES), BF16),
            pltpu.VMEM((2, rows, LANES), BF16),
            pltpu.VMEM((2, rows, LANES), BF16),
            dma((2,)),
            dma((2,)),
            pltpu.VMEM((2, rows, LANES), F32),
            pltpu.VMEM((groups, 2, 2 * mem_here, levels, LANES), F32),
            pltpu.VMEM((blocks, rows, LANES), F32),
            pltpu.VMEM((levels * levels, own), F32),
            pltpu.VMEM(piece, BF16),
            pltpu.VMEM(piece, BF16),
            dma((groups,)),
            dma((groups,)),
            pltpu.VMEM(piece, BF16),
            dma((groups,)),
            dma((groups,)),
            pltpu.VMEM((blocks, rows, LANES), F32),
            pltpu.VMEM((2, rows, LANES), BF16),
            pltpu.VMEM((2, rows, LANES), BF16),
            dma((2,)),
            dma((2,)),
        ],
        compiler_params=pltpu.CompilerParams(
            collective_id=0, has_side_effects=True, vmem_limit_bytes=VMEM_GRANT
        ),
        name="hessian_step",
    )(*args)
    return pl.pallas_call(
        hand_over,
        out_shape=out_shape,
        in_specs=[pl.BlockSpec(memory_space=pltpu.VMEM)] * 2,
        out_specs=[pl.BlockSpec(memory_space=pl.ANY)] * 2,
        scratch_shapes=[dma((mem_here + 1,))],
        compiler_params=pltpu.CompilerParams(vmem_limit_bytes=VMEM_GRANT),
        name="hand_over",
    )(*results)


def solution(mesh):
    placed = (
        P("member", None, "patch"),
        P("member", None, "patch"),
        P(None, "patch", None, None),
        P("patch", None, None),
        P("patch"),
        P("patch", None),
        P("patch", None),
        P("patch", "member"),
        P("patch", None, "member"),
        P("patch", "member"),
        P("patch", "member"),
    )
    return jax.shard_map(
        per_device,
        mesh=mesh,
        in_specs=placed,
        out_specs=(P("member", None, "patch"), P(None, ("patch", "member"))),
        check_vma=False,
    )
```

```python
import functools
import math

import jax
import jax.numpy as jnp
from jax import lax
from jax.experimental import pallas as pl
from jax.experimental.pallas import tpu as pltpu
from jax.sharding import PartitionSpec as P

F32 = jnp.float32
BF16 = jnp.bfloat16
LANES = 128
VMEM_GRANT = 48 << 20
MESH = pl.DeviceIdType.MESH


def dot_nt(x, w):
    return lax.dot_general(x, w, (((1,), (1,)), ((), ())), preferred_element_type=F32)


def dot_nn(x, w):
    return lax.dot_general(x, w, (((1,), (0,)), ((), ())), preferred_element_type=F32)


def table(rows, base, count):
    node = lax.broadcasted_iota(jnp.int32, (count, rows.shape[1]), 0) + base
    return jnp.where(node == rows, 1.0, 0.0).astype(BF16)


def split_bf16(x):
    high = x.astype(BF16)
    return high, (x - high.astype(F32)).astype(BF16)


def kernel(
    groups,
    depth,
    patches,
    control_h,
    members_h,
    conv_h,
    interp_h,
    source_h,
    right_h,
    left_h,
    cells_h,
    weights_h,
    precision_h,
    count_h,
    product_v,
    inc_v,
    control_v,
    members_v,
    conv_v,
    interp_v,
    source_s,
    right_v,
    left_v,
    cells_v,
    weights_v,
    precision_v,
    count_s,
    load_sem,
    row_sem,
    right_table,
    left_table,
    halo_send,
    halo_recv,
    halo_send_sem,
    halo_recv_sem,
    edge_acc,
    edge_members,
    conv_f,
    obs_a,
    part,
    arrived,
    part_send_sem,
    part_recv_sem,
    sens,
    sens_send_sem,
    sens_recv_sem,
    nodal,
    give,
    got,
    give_send_sem,
    give_recv_sem,
):
    me = lax.axis_index("member")
    patch = lax.axis_index("patch")
    width = groups // depth
    my_row, my_col = me // depth, lax.rem(me, depth)
    upper, lower = lax.rem(patch + 1, patches), lax.rem(patch + patches - 1, patches)
    mem_here, levels, node_count = control_v.shape
    rows = mem_here * levels
    blocks = node_count // LANES
    edge = 2 * LANES
    factor = 1.0 / math.sqrt(mem_here * groups - 1)
    near = sorted(range(depth), key=lambda d: (min(d, depth - d), d))
    far = near[::-1]

    mirrored = my_row * 2 >= width
    inward = jnp.where(mirrored, width - 1 - my_row, my_row)

    def row_at(turn):
        straight = jnp.where(
            turn < 2, width - 1 - turn, jnp.where(turn == 2, 1 - inward, inward)
        )
        if width < 4:
            straight = lax.rem(my_row + width - 1 - turn, width)
            return straight
        return jnp.where(mirrored, width - 1 - straight, straight)

    def peer(row, step):
        return row * depth + lax.rem(my_col + step, depth)

    def each_far(body):
        lax.fori_loop(0, width, lambda t, carry: (body(row_at(t)), carry)[1], 0)

    def each_near(body, carry=0):
        return lax.fori_loop(0, width, lambda t, c: body(row_at(width - 1 - t), c), carry)

    def unless_me(row, step, act):
        if step == 0:
            pl.when(row != my_row)(act)
        else:
            act()

    barrier = pltpu.get_barrier_semaphore()

    def across(turn):
        return lax.rem(my_row + turn, width) * depth + my_col

    def greet(semaphore, m):
        pl.semaphore_signal(semaphore, inc=1, device_id=(m, patch), device_id_type=MESH)

    for other in (upper, lower):
        pl.semaphore_signal(barrier, inc=1, device_id=(me, other), device_id_type=MESH)
    for step in far[:-1]:
        greet(barrier, peer(my_row, step))
    for turn in range(1, width):
        greet(barrier, across(turn))

    sources = (control_h, right_h, left_h, source_h, conv_h, weights_h, precision_h, cells_h, count_h, interp_h, members_h)
    targets = (control_v, right_v, left_v, source_s, conv_v, weights_v, precision_v, cells_v, count_s, interp_v, members_v)
    loads = [
        pltpu.make_async_copy(a, b, load_sem.at[i]) for i, (a, b) in enumerate(zip(sources, targets))
    ]
    for load in loads:
        load.start()

    def node_block(b):
        return control_v[:, :, b * LANES : (b + 1) * LANES].reshape(rows, LANES).astype(BF16)

    for load in loads[:3]:
        load.wait()
    right_table[...] = table(right_v[...], node_count - edge, edge)
    left_table[...] = table(left_v[...], 0, edge)
    last = jnp.concatenate([node_block(blocks - 2), node_block(blocks - 1)], axis=1)
    first = jnp.concatenate([node_block(0), node_block(1)], axis=1)
    halo_send[0] = dot_nn(last, right_table[...]).astype(BF16)
    halo_send[1] = dot_nn(first, left_table[...]).astype(BF16)

    pl.semaphore_wait(barrier, depth + width)

    def halo_copy(i, other):
        return pltpu.make_async_remote_copy(
            src_ref=halo_send.at[i],
            dst_ref=halo_recv.at[i],
            send_sem=halo_send_sem.at[i],
            recv_sem=halo_recv_sem.at[i],
            device_id=(me, other),
            device_id_type=MESH,
        )

    halos = [halo_copy(0, upper), halo_copy(1, lower)]
    for copy in halos:
        copy.start()
    for turn in range(1, width):
        greet(row_sem, across(turn))

    for load in loads[3:5]:
        load.wait()
    for b in range(blocks):
        acc = dot_nt(node_block(b), conv_v[0, b])
        if b > 0:
            acc = acc + dot_nt(node_block(b - 1), conv_v[1, b])
        if b < blocks - 1:
            acc = acc + dot_nt(node_block(b + 1), conv_v[2, b])
        if b == 0:
            edge_acc[0] = acc
        elif b == blocks - 1:
            edge_acc[1] = acc
        else:
            conv_f[b] = acc.astype(BF16).astype(F32)

    for load in loads[5:9]:
        load.wait()
    slots = cells_v.shape[1]
    own = 2 * LANES
    live = lax.broadcasted_iota(jnp.int32, (1, slots), 1) < count_s[0, 0]
    scaled = jnp.where(live, precision_v[...], 0.0)
    level_w = weights_v[0]
    outer = jnp.concatenate(
        [level_w * (level_w[l : l + 1] * scaled) for l in range(levels)], axis=0
    )
    place = table(cells_v[...], 0, own)
    high, low = split_bf16(outer)
    obs_a[...] = dot_nt(high, place) + dot_nt(low, place)

    for load in loads[9:]:
        load.wait()

    def members_at(c):
        here = members_v[:, :, pl.ds(pl.multiple_of(c * LANES, LANES), LANES)]
        return here.astype(F32)

    def mark_edges(m, carry):
        for h in range(2):
            c = m * 2 + h
            scaled_members = members_at(c) * factor
            at = jnp.full(scaled_members.shape, source_s[c], jnp.int32)
            marked = jnp.stack(
                [jnp.where(at == b, scaled_members, 0.0) for b in (0, blocks - 1)]
            )
            edge_members[m, h] = marked.reshape(2 * mem_here, levels, LANES)
        return carry

    lax.fori_loop(0, groups, mark_edges, 0)

    for copy in halos:
        copy.wait_recv()
    conv_f[0] = (edge_acc[0] + dot_nt(halo_recv[0], conv_v[1, 0])).astype(BF16).astype(F32)
    conv_f[blocks - 1] = (
        (edge_acc[1] + dot_nt(halo_recv[1], conv_v[2, blocks - 1])).astype(BF16).astype(F32)
    )

    def part_copy(m, landing):
        return pltpu.make_async_remote_copy(
            src_ref=part.at[m],
            dst_ref=arrived.at[landing],
            send_sem=part_send_sem.at[m],
            recv_sem=part_recv_sem.at[0],
            device_id=(m, patch),
            device_id_type=MESH,
        )

    def both(first, second):
        none = jnp.zeros_like(first)
        upper_rows = jnp.concatenate([first, none], axis=1)
        return jnp.concatenate(
            [upper_rows, jnp.concatenate([none, second], axis=1)], axis=0
        ).astype(BF16)

    def forward(row):
        for batch in (far[: depth // 2], far[depth // 2 :]):
            for step in batch:
                m = peer(row, step)
                c = m * 2
                picked = both(conv_f[source_s[c]], conv_f[source_s[c + 1]])
                weights = jnp.concatenate([interp_v[c], interp_v[c + 1]], axis=1)
                field = dot_nt(picked, weights).reshape(2, mem_here, levels, LANES)
                perturb = jnp.stack([members_at(c), members_at(c + 1)])
                inc_part = jnp.sum(field * perturb, axis=1)
                part[m] = inc_part.reshape(2 * levels, LANES).astype(BF16)
            for step in batch:
                unless_me(row, step, lambda: part_copy(peer(row, step), me).start())

    pl.semaphore_wait(row_sem, width - 1)
    each_far(forward)

    others = pl.ds(0, groups - 1)
    pltpu.make_async_copy(arrived.at[others], arrived.at[others], part_recv_sem.at[0]).wait()
    arrived[me] = part[me]
    sums = [arrived[m].astype(F32) for m in range(groups)]
    while len(sums) > 1:
        sums = [a + b for a, b in zip(sums[::2], sums[1::2])]
    total = sums[0]
    inc = total * factor

    pieces = []
    for h in range(2):
        half = inc[h * levels : (h + 1) * levels]
        inc_v[:, h * LANES : (h + 1) * LANES] = half
        acc = None
        for l in range(levels):
            term = (
                obs_a[l * levels : (l + 1) * levels, h * LANES : (h + 1) * LANES]
                * half[l : l + 1]
            )
            acc = term if acc is None else acc + term
        pieces.append(acc)
    sens[me] = jnp.concatenate(pieces, axis=0).astype(BF16)

    def sens_copy(m, landing):
        return pltpu.make_async_remote_copy(
            src_ref=sens.at[landing],
            dst_ref=sens.at[landing],
            send_sem=sens_send_sem.at[m],
            recv_sem=sens_recv_sem.at[landing],
            device_id=(m, patch),
            device_id_type=MESH,
        )

    def share(row):
        for step in far:
            unless_me(row, step, lambda: sens_copy(peer(row, step), me).start())

    each_far(share)

    def weights_of(m):
        return jnp.concatenate([interp_v[m * 2], interp_v[m * 2 + 1]], axis=0)

    def edges(row, total):
        for pair in range(0, depth, 8):
            peers = [peer(row, step) for step in near[pair : pair + 8]]
            for step, m in zip(near[pair : pair + 8], peers):
                unless_me(row, step, lambda: sens_copy(m, m).wait_recv())
            added = []
            for m in peers:
                there = sens[m].astype(F32)
                marked = jnp.concatenate(
                    [
                        (edge_members[m, h] * there[h * levels : (h + 1) * levels][None]).reshape(
                            2 * rows, LANES
                        )
                        for h in range(2)
                    ],
                    axis=1,
                )
                added.append(dot_nn(marked.astype(BF16), weights_of(m)))
            while len(added) > 1:
                added = [a + b for a, b in zip(added[::2], added[1::2])]
            total = total + added[0]
        return total

    ends = each_near(edges, jnp.zeros((2 * rows, LANES), F32)).astype(BF16)

    def give_copy(i, other):
        return pltpu.make_async_remote_copy(
            src_ref=give.at[i],
            dst_ref=got.at[i],
            send_sem=give_send_sem.at[i],
            recv_sem=give_recv_sem.at[i],
            device_id=(me, other),
            device_id_type=MESH,
        )

    give[0] = dot_nn(ends[:rows], conv_v[1, 0]).astype(BF16)
    give[1] = dot_nn(ends[rows:], conv_v[2, blocks - 1]).astype(BF16)
    gifts = [give_copy(0, lower), give_copy(1, upper)]
    for copy in gifts:
        copy.start()

    nodal[...] = jnp.zeros_like(nodal)
    nodal[0] = ends[:rows].astype(F32)
    nodal[blocks - 1] = ends[rows:].astype(F32)

    chunk = min(groups, 8)

    def backward(turn, carry):
        for pair in range(0, chunk, 2):
            spread = []
            for k in range(2):
                m = turn * chunk + pair + k
                there = sens[m].astype(F32) * factor
                adjoint = [
                    (members_at(m * 2 + h) * there[h * levels : (h + 1) * levels][None]).reshape(
                        rows, LANES
                    )
                    for h in range(2)
                ]
                value = dot_nn(both(*adjoint), weights_of(m))
                for h in range(2):
                    at = jnp.full((rows, LANES), source_s[m * 2 + h], jnp.int32)
                    spread.append((at, value[h * rows : (h + 1) * rows]))
            for b in range(1, blocks - 1):
                acc = nodal[b]
                for at, value in spread:
                    acc = acc + jnp.where(at == b, value, 0.0)
                nodal[b] = acc
        return carry

    lax.fori_loop(0, groups // chunk, backward, 0)

    def node_adjoint(b):
        return nodal[b].astype(BF16)

    for b in range(blocks):
        acc = dot_nn(node_adjoint(b), conv_v[0, b])
        if b < blocks - 1:
            acc = acc + dot_nn(node_adjoint(b + 1), conv_v[1, b + 1])
        if b > 0:
            acc = acc + dot_nn(node_adjoint(b - 1), conv_v[2, b - 1])
        span = slice(b * LANES, (b + 1) * LANES)
        product_v[:, :, span] = control_v[:, :, span] + acc.reshape(mem_here, levels, LANES)

    def drain(row):
        for step in near:
            m = peer(row, step)

            def sent():
                part_copy(m, me).wait_send()
                sens_copy(m, me).wait_send()

            unless_me(row, step, sent)

    each_far(drain)

    for copy in gifts:
        copy.wait_recv()
    for i, (tab, start) in enumerate(((right_table, node_count - edge), (left_table, 0))):
        added = dot_nt(got[i], tab[...]).reshape(mem_here, levels, edge)
        span = slice(start, start + edge)
        product_v[:, :, span] = product_v[:, :, span] + added

    for copy in halos + gifts:
        copy.wait_send()


def hand_over(product_v, inc_v, product_h, inc_h, sem):
    outs = [pltpu.make_async_copy(inc_v, inc_h, sem.at[0])]
    for k in range(product_v.shape[0]):
        outs.append(pltpu.make_async_copy(product_v.at[k], product_h.at[k], sem.at[k + 1]))
    for out in outs:
        out.start()
    for out in outs:
        out.wait()


def per_device(*args):
    args = [pltpu.with_memory_space_constraint(a, pltpu.HBM) for a in args[:-1]] + [args[-1]]
    control, members, conv_blocks, interp = args[:4]
    groups, patches = lax.axis_size("member"), lax.axis_size("patch")
    depth = 8 if groups % 8 == 0 else 2
    mem_here, levels, node_count = control.shape
    rows = mem_here * levels
    blocks = node_count // LANES
    slots = args[7].shape[1]
    own = 2 * LANES
    smem = (4, 10)
    loaded = [
        (pltpu.SMEM if i in smem else pltpu.VMEM)(a.shape, a.dtype) for i, a in enumerate(args)
    ]
    dma = pltpu.SemaphoreType.DMA
    piece = (groups, 2 * levels, LANES)
    out_shape = (
        jax.ShapeDtypeStruct(control.shape, F32),
        jax.ShapeDtypeStruct((levels, own), F32),
    )
    results = pl.pallas_call(
        functools.partial(kernel, groups, depth, patches),
        out_shape=tuple(pltpu.VMEM(a.shape, a.dtype) for a in out_shape),
        in_specs=[pl.BlockSpec(memory_space=pltpu.HBM)] * len(args),
        out_specs=[pl.BlockSpec(memory_space=pltpu.VMEM)] * 2,
        scratch_shapes=loaded
        + [
            dma((len(args),)),
            pltpu.SemaphoreType.REGULAR,
            pltpu.VMEM((own, LANES), BF16),
            pltpu.VMEM((own, LANES), BF16),
            pltpu.VMEM((2, rows, LANES), BF16),
            pltpu.VMEM((2, rows, LANES), BF16),
            dma((2,)),
            dma((2,)),
            pltpu.VMEM((2, rows, LANES), F32),
            pltpu.VMEM((groups, 2, 2 * mem_here, levels, LANES), F32),
            pltpu.VMEM((blocks, rows, LANES), F32),
            pltpu.VMEM((levels * levels, own), F32),
            pltpu.VMEM(piece, BF16),
            pltpu.VMEM(piece, BF16),
            dma((groups,)),
            dma((groups,)),
            pltpu.VMEM(piece, BF16),
            dma((groups,)),
            dma((groups,)),
            pltpu.VMEM((blocks, rows, LANES), F32),
            pltpu.VMEM((2, rows, LANES), BF16),
            pltpu.VMEM((2, rows, LANES), BF16),
            dma((2,)),
            dma((2,)),
        ],
        compiler_params=pltpu.CompilerParams(
            collective_id=0, has_side_effects=True, vmem_limit_bytes=VMEM_GRANT
        ),
        name="hessian_step",
    )(*args)
    return pl.pallas_call(
        hand_over,
        out_shape=out_shape,
        in_specs=[pl.BlockSpec(memory_space=pltpu.VMEM)] * 2,
        out_specs=[pl.BlockSpec(memory_space=pl.ANY)] * 2,
        scratch_shapes=[dma((mem_here + 1,))],
        compiler_params=pltpu.CompilerParams(vmem_limit_bytes=VMEM_GRANT),
        name="hand_over",
    )(*results)


def solution(mesh):
    placed = (
        P("member", None, "patch"),
        P("member", None, "patch"),
        P(None, "patch", None, None),
        P("patch", None, None),
        P("patch"),
        P("patch", None),
        P("patch", None),
        P("patch", "member"),
        P("patch", None, "member"),
        P("patch", "member"),
        P("patch", "member"),
    )
    return jax.shard_map(
        per_device,
        mesh=mesh,
        in_specs=placed,
        out_specs=(P("member", None, "patch"), P(None, ("patch", "member"))),
        check_vma=False,
    )
```
